256 devices in a mesh: leaf: 64 (over z, x, core), sub: 4 (over y).
Axes of the slice: x: 4, y: 4, z: 8, core: 2. Of those that a mesh axis runs over, the one named last changes fastest.
Arguments:
- coords: bfloat16 [32768, 3, 128], P('leaf'), may hold values from 0 to 4
- charges: bfloat16 [32768, 8, 128], P(('leaf', 'sub')), may hold values from -6 to 6
- counts: int32 [32768], P('leaf'), may hold values from 32 to 128, as said below
- morton: int32 [32768], P('leaf'), may hold values from 0 to 511, as said below
- near_list: int32 [32768, 27], P(('leaf', 'sub')), may hold values from -1 to 32767, as said below
- basis: bfloat16 [32768, 64, 128], P(('leaf', 'sub')), may hold values from -0.5 to 0.5
- transfer1: bfloat16 [32768, 64, 64], P(('leaf', 'sub')), may hold values from -0.75 to 0.75
- far2_list: int32 [4096, 16], P(('leaf', 'sub')), may hold values from -1 to 4095, as said below
- coupling2: bfloat16 [4096, 16, 64, 64], P(('leaf', 'sub')), may hold values from -0.0625 to 0.0625
- transfer2: bfloat16 [4096, 64, 64], P('leaf'), may hold values from -0.75 to 0.75
- far3_list: int32 [64, 8], P('leaf'), may hold values from -1 to 63, as said below
- coupling3: bfloat16 [64, 8, 64, 64], P('leaf'), may hold values from -0.01171875 to 0.01171875
Outputs:
- potential: float32 [32768, 8, 128], P(('leaf', 'sub'))
The draws below stay inside these ranges and needn't reach their ends.
Inputs may be any that keep to these rules, and one draw needn't show every extreme that they name: `counts`: each leaf's number of live points; leaves do not all have the same number. `morton`: within every block of 512 consecutive entries, a permutation of 0 to 511. `near_list`: row t starts with t itself; its other live entries are leaves other than t in the leaf group of t or in the group just before or after it; live entries come first and -1 fills the rest, with at least 13 live entries a row; entries may repeat. `far2_list`: row b names boxes other than b in the leaf group of b or in the group just before or after it; live entries come first and -1 fills the rest, with at least 8 live entries a row; entries may repeat. `far3_list`: row q names group boxes other than q; live entries come first and -1 fills the rest, with at least 4 live entries a row; entries may repeat.
All inputs are finite; a program needn't handle non-finite values.
Results may differ from the reference program's by a relative error of at most 0.011.
Values may be sent and summed in bfloat16 or wider, within the bound.
No kernel may reach another device: no remote copies, remote signals or barrier semaphores. Data moves between devices by JAX's collectives and lax.ppermute only.
A program may use at most 64 MiB of HBM per device.

```python
import jax
import jax.numpy as jnp
from jax import lax

PTS = 128
RANK = 64
RHS = 8
NEAR = 27
FAR2 = 16
FAR3 = 8
GROUP = 512
LEAVES = 32768
BOXES2 = 4096
BOXES3 = 64


def window_list(key, items, per_group, slots, keep_self, forced_item):
    index = jnp.arange(items, dtype=jnp.int32)
    owner = index // per_group
    groups = items // per_group
    lower = jnp.maximum(owner - 1, 0) * per_group
    upper = jnp.minimum(owner + 2, groups) * per_group
    pick_key, count_key = jax.random.split(key)
    raw = jax.random.randint(pick_key, (items, slots), 0, 1 << 20).astype(jnp.int32)
    picked = lower[:, None] + raw % (upper - lower - 1)[:, None]
    picked = jnp.where(picked >= index[:, None], picked + 1, picked)
    if keep_self:
        picked = picked.at[:, 0].set(index)
    else:
        picked = picked.at[forced_item, 0].set(items - 1)
    least = slots // 2
    live = least + jax.random.randint(count_key, (items,), 0, slots - least + 1).astype(jnp.int32)
    live = live.at[0].set(least)
    slot = jnp.arange(slots, dtype=jnp.int32)
    return jnp.where(slot[None, :] < live[:, None], picked, -1).astype(jnp.int32)


def draw_counts(key, part):
    values = jax.random.randint(key, (LEAVES,), PTS // 4, PTS + 1).astype(jnp.int32)
    return values.at[0].set(PTS).at[1].set(PTS // 4)


def group_order(key):
    return jax.random.permutation(key, GROUP).astype(jnp.int32)


def draw_morton(key, part):
    keys = jax.random.split(key, LEAVES // GROUP)
    return jax.vmap(group_order)(keys).reshape(LEAVES).astype(jnp.int32)


def draw_near_list(key, part):
    return window_list(key, LEAVES, GROUP, NEAR, True, 0)


def draw_far2_list(key, part):
    return window_list(key, BOXES2, BOXES2 // BOXES3, FAR2, False, BOXES2 - 2)


def draw_far3_list(key, part):
    return window_list(key, BOXES3, BOXES3, FAR3, False, 0)


def block_levels(own_key, shape, cuts, smallest, top_value):
    def one(axis_at, blocks):
        draws = jax.random.uniform(jax.random.fold_in(jax.random.fold_in(own_key, 6), axis_at), (blocks,), jnp.float32, smallest / len(cuts), top_value / len(cuts))
        return jnp.repeat(jnp.exp(draws), shape[axis_at] // blocks).reshape((-1,) + (1,) * (len(shape) - axis_at - 1))

    gain = one(*cuts[0])
    for cut in cuts[1:]:
        gain = gain * one(*cut)
    return gain


def gaussian(stream_key, extent, scale, most, cuts=(), kind=jnp.bfloat16):
    array = scale * jax.random.normal(stream_key, extent, jnp.float32)
    if cuts:
        array = array * block_levels(stream_key, extent, cuts, -0.22, 0.18)
    return jnp.clip(array, -most, most).astype(kind)


def setup_inputs(seed: int = 0) -> dict:
    streams_of = jax.random.split(jax.random.key(seed), 13)
    coords = jnp.clip(4.0 * jax.random.uniform(streams_of[0], (LEAVES, 3, PTS), jnp.float32) ** block_levels(streams_of[0], (LEAVES, 3, PTS), ((0, 64),), -0.2, 0.2), 0.0, 4.0).astype(jnp.bfloat16)
    charges = gaussian(streams_of[1], (LEAVES, RHS, PTS), 1.0, 6.0, ((0, 256),))
    counts = draw_counts(jax.random.fold_in(streams_of[12], 71), 0)
    morton = draw_morton(jax.random.fold_in(streams_of[12], 71), 0)
    near_list = draw_near_list(jax.random.fold_in(streams_of[12], 71), 0)
    basis = gaussian(streams_of[5], (LEAVES, RANK, PTS), PTS ** -0.5, 0.5, ((0, 256),))
    transfer1 = gaussian(streams_of[6], (LEAVES, RANK, RANK), RANK ** -0.5, 0.75, ((0, 256),))
    far2_list = draw_far2_list(jax.random.fold_in(streams_of[12], 71), 0)
    coupling2 = gaussian(streams_of[8], (BOXES2, FAR2, RANK, RANK), (RANK * FAR2 * 8) ** -0.5, 0.0625, ((0, 256),))
    transfer2 = gaussian(streams_of[9], (BOXES2, RANK, RANK), RANK ** -0.5, 0.75, ((0, 64),))
    far3_list = draw_far3_list(jax.random.fold_in(streams_of[12], 71), 0)
    coupling3 = gaussian(streams_of[11], (BOXES3, FAR3, RANK, RANK), (RANK * FAR3 * GROUP) ** -0.5, 0.01171875, ((0, 64),))
    return {"coords": coords, "charges": charges, "counts": counts, "morton": morton, "near_list": near_list, "basis": basis, "transfer1": transfer1, "far2_list": far2_list, "coupling2": coupling2, "transfer2": transfer2, "far3_list": far3_list, "coupling3": coupling3}


kernel_scale = 0.07957747154594767
delta_squared = 0.0025

def kernel_tile(targets, sources):
    squared = jnp.zeros((targets.shape[0], targets.shape[2], sources.shape[2]), jnp.float32)
    for component in range(3):
        offset = targets[:, component, :, None] - sources[:, component, None, :]
        squared = squared + offset * offset
    return (kernel_scale / jnp.sqrt(squared + delta_squared)).astype(jnp.bfloat16)

def far_field(moments, lists, couplings):
    valid = lists >= 0
    source = moments[jnp.maximum(lists, 0)].astype(jnp.float32)
    source = jnp.where(valid[..., None, None], source, jnp.zeros_like(source))
    return jnp.einsum('bkrc,bkcp->brp', source, couplings.astype(jnp.float32))

def reference(coords, charges, counts, morton, near_list, basis, transfer1, far2_list, coupling2, transfer2, far3_list, coupling3):
    leaf_ids = jnp.arange(LEAVES, dtype=jnp.int32)
    target_slot = leaf_ids // GROUP * GROUP + morton
    ordered = jnp.zeros_like(charges).at[target_slot].set(charges)
    live = jnp.arange(PTS, dtype=jnp.int32)[None, :] < counts[:, None]
    masked = jnp.where(live[:, None, :], ordered, jnp.zeros_like(ordered))
    leaf_moments = jnp.einsum('trp,tkp->trk', masked.astype(jnp.float32), basis.astype(jnp.float32)).astype(jnp.bfloat16)
    child_terms = jnp.einsum('trc,tcp->trp', leaf_moments.astype(jnp.float32), transfer1.astype(jnp.float32))
    box_moments = child_terms.reshape(BOXES2, 8, RHS, RANK).sum(axis=1).astype(jnp.bfloat16)
    box_terms = jnp.einsum('brc,bcp->brp', box_moments.astype(jnp.float32), transfer2.astype(jnp.float32))
    group_moments = box_terms.reshape(BOXES3, BOXES2 // BOXES3, RHS, RANK).sum(axis=1).astype(jnp.bfloat16)
    top_field = far_field(group_moments, far3_list, coupling3).astype(jnp.bfloat16)
    box_far = far_field(box_moments, far2_list, coupling2)
    parent_field = jnp.repeat(top_field, BOXES2 // BOXES3, axis=0).astype(jnp.float32)
    box_local = (box_far + jnp.einsum('brp,bcp->brc', parent_field, transfer2.astype(jnp.float32))).astype(jnp.bfloat16)
    spread = jnp.repeat(box_local, 8, axis=0).astype(jnp.float32)
    leaf_local = jnp.einsum('trp,tcp->trc', spread, transfer1.astype(jnp.float32)).astype(jnp.bfloat16)
    far_part = jnp.einsum('trk,tkp->trp', leaf_local.astype(jnp.float32), basis.astype(jnp.float32))
    coords_float = coords.astype(jnp.float32)

    def near_group(group):
        start = (group * GROUP).astype(jnp.int32)
        targets = lax.dynamic_slice_in_dim(coords_float, start, GROUP, 0)
        lists = lax.dynamic_slice_in_dim(near_list, start, GROUP, 0)

        def slot_step(total, column):
            valid = column >= 0
            index = jnp.maximum(column, 0)
            tile = kernel_tile(targets, coords_float[index]).astype(jnp.float32)
            source = masked[index].astype(jnp.float32)
            source = jnp.where(valid[:, None, None], source, jnp.zeros_like(source))
            return (total + jnp.einsum('tij,trj->tri', tile, source), None)
        total, unused = lax.scan(slot_step, jnp.zeros((GROUP, RHS, PTS), jnp.float32), lists.T)
        return total
    near_part = lax.map(near_group, jnp.arange(BOXES3, dtype=jnp.int32)).reshape(LEAVES, RHS, PTS)
    summed = near_part + far_part
    return jnp.where(live[:, None, :], summed, jnp.zeros_like(summed))
```

```python
import functools

import jax
import jax.numpy as jnp
from jax import lax
from jax.experimental import pallas as pl
from jax.experimental.pallas import tpu as pltpu
from jax.sharding import PartitionSpec as P

kernel_scale = 0.07957747154594767
delta_squared = 0.0025

SLOTS = 4
UNITS = 8
STRIDE = 32
CLASSES = (64, 96, 128)


def shift(x, axis, by):
    count = lax.axis_size(axis)
    return lax.ppermute(x, axis, [(i, (i + by) % count) for i in range(count)])


def slide(x, axis, by):
    count = lax.axis_size(axis)
    pairs = [(i, i + by) for i in range(count) if 0 <= i + by < count]
    return lax.ppermute(x, axis, pairs)


def gather_ring(x, axis):
    count = lax.axis_size(axis)
    return [x] + [shift(x, axis, -k) for k in range(1, count)]


def near_kernel(
    words,
    lists,
    places,
    bounds,
    own_coords,
    left_c,
    mid_c,
    right_c,
    left_q,
    mid_q,
    right_q,
    out_ref,
    tile_t,
    src_c,
    src_q,
    acc,
    sems,
):
    bf = jnp.bfloat16
    group = mid_q.shape[0]
    targets = out_ref.shape[0]
    copies = []
    for k, (c, q) in enumerate(((left_c, left_q), (mid_c, mid_q), (right_c, right_q))):
        rows = pl.ds(k * group, group)
        copies.append(pltpu.make_async_copy(c, src_c.at[rows], sems.at[k, 0]))
        copies.append(pltpu.make_async_copy(q, src_q.at[rows], sems.at[k, 1]))
    for copy in copies:
        copy.start()
    src_c[3 * group] = jnp.zeros(src_c.shape[1:], src_c.dtype)
    src_q[3 * group] = jnp.zeros(src_q.shape[1:], src_q.dtype)

    def prepare(w, _):
        for j in range(8):
            t = w * 8 + j
            x = own_coords[t]
            for c in range(3):
                tile_t[t * 3 + c] = jnp.broadcast_to(x[c : c + 1, :], (128, 128)).T
        return 0

    lax.fori_loop(0, targets // 8, prepare, 0)
    for c in range(3):
        tile_t[targets * 3 + c] = jnp.zeros((128, 128), jnp.float32)
    acc[...] = jnp.zeros_like(acc)
    for copy in copies:
        copy.wait()

    def unit(word, rows):
        t = lax.shift_right_logical(word, 5)
        ids = [lists[word + k] for k in range(SLOTS)]
        charge = jnp.concatenate([src_q[places[i]] for i in ids], axis=1)
        target = [
            [tile_t[t * 3 + c, 16 * m : 16 * m + 16, :].astype(bf) for c in range(3)]
            for m in range(rows // 16)
        ]
        columns = []
        for i in ids:
            source = [
                jnp.broadcast_to(src_c[i, c : c + 1, :], (16, 128)).astype(bf) for c in range(3)
            ]
            pieces = []
            for m in range(rows // 16):
                squared = None
                for c in range(3):
                    offset = target[m][c] - source[c]
                    if squared is None:
                        squared = offset * offset + jnp.asarray(delta_squared, bf)
                    else:
                        squared = squared + offset * offset
                pieces.append(lax.rsqrt(squared))
            columns.append(jnp.concatenate(pieces, axis=0))
        tile = jnp.concatenate(columns, axis=1)
        return t, lax.dot_general(
            charge, tile, (((1,), (1,)), ((), ())), preferred_element_type=jnp.float32
        )

    def step(rows, w, _):
        done = [unit(words[w * UNITS + j], rows) for j in range(UNITS)]
        for t, part in done:
            if rows < 128:
                part = jnp.concatenate([part, jnp.zeros((8, 128 - rows), jnp.float32)], axis=1)
            acc[t] = acc[t] + part * kernel_scale
        return 0

    for k, rows in enumerate(CLASSES):
        lax.fori_loop(bounds[k], bounds[k + 1], functools.partial(step, rows), 0)
    out_ref[...] = acc[:targets]


def near_field(words, lists, places, bounds, own_coords, coords, charges):
    targets = own_coords.shape[0]
    group = coords[0].shape[0]
    whole = pl.BlockSpec(memory_space=pl.ANY)
    return pl.pallas_call(
        near_kernel,
        out_shape=jax.ShapeDtypeStruct((targets, 8, 128), jnp.float32),
        grid_spec=pltpu.PrefetchScalarGridSpec(
            num_scalar_prefetch=4,
            grid=(),
            in_specs=[pl.BlockSpec(memory_space=pltpu.VMEM)] + [whole] * 6,
            out_specs=pl.BlockSpec(memory_space=pltpu.VMEM),
            scratch_shapes=[
                pltpu.VMEM((targets * 3 + 3, 128, 128), jnp.float32),
                pltpu.VMEM((3 * group + 1, 4, 128), jnp.float32),
                pltpu.VMEM((3 * group + 1, 8, 128), jnp.bfloat16),
                pltpu.VMEM((targets + 1, 8, 128), jnp.float32),
                pltpu.SemaphoreType.DMA((3, 2)),
            ],
        ),
        compiler_params=pltpu.CompilerParams(vmem_limit_bytes=56 << 20),
        cost_estimate=pl.CostEstimate(
            flops=1 << 30, bytes_accessed=12 << 20, transcendentals=50 << 20
        ),
        name="near_field",
    )(words, lists, places, bounds, own_coords, *coords, *charges)


def plan_units(near_list, base, group, counts):
    targets, slots = near_list.shape
    dummy = 3 * group
    live = near_list >= 0
    local = jnp.where(live, jnp.clip(near_list - base, 0, dummy - 1), dummy)
    lists = jnp.full((targets + 1, STRIDE), dummy, jnp.int32)
    lists = lax.dynamic_update_slice(lists, local, (0, 0))
    number = (jnp.sum(live, axis=1, dtype=jnp.int32) + SLOTS - 1) // SLOTS
    kind = sum((counts > rows).astype(jnp.int32) for rows in CLASSES[:-1])
    classes = jnp.arange(len(CLASSES), dtype=jnp.int32)
    total = jnp.sum(jnp.where(kind[None, :] == classes[:, None], number[None, :], 0), axis=1)
    steps = (total + UNITS - 1) // UNITS
    first = jnp.sum(
        jnp.where(classes[None, :] < classes[:, None], steps[None, :], 0), axis=1
    )
    bounds = jnp.concatenate([first, (first[-1] + steps[-1])[None]])
    ids = jnp.arange(targets, dtype=jnp.int32)
    before = (kind[None, :] == kind[:, None]) & (ids[None, :] < ids[:, None])
    start = jnp.sum(jnp.where(before, number[None, :], 0), axis=1) + UNITS * jnp.sum(
        jnp.where(kind[:, None] == classes[None, :], first[None, :], 0), axis=1
    )
    most = targets * ((slots + SLOTS - 1) // SLOTS) + UNITS * len(CLASSES)
    unit = jnp.arange(most, dtype=jnp.int32)
    at = unit[:, None] - start[None, :]
    mine = (at >= 0) & (at < number[None, :])
    word = jnp.sum(
        jnp.where(mine, ids[None, :] * STRIDE + at * SLOTS - targets * STRIDE, 0), axis=1
    )
    return word + targets * STRIDE, lists.reshape(-1), bounds


def far_field(moments, lists, couplings, offset):
    valid = lists >= 0
    local = jnp.clip(lists - offset, 0, moments.shape[0] - 1)
    source = jnp.where(valid[..., None, None], moments[local], jnp.zeros((), moments.dtype))
    return jnp.einsum("bkrc,bkcp->brp", source, couplings, preferred_element_type=jnp.float32)


def on_device(
    coords,
    charges,
    counts,
    morton,
    near_list,
    basis,
    transfer1,
    far2_list,
    coupling2,
    transfer2,
    far3_list,
    coupling3,
):
    lane = lax.axis_index("sub")
    group = lax.axis_index("leaf")
    leaves = lax.axis_size("leaf")
    lanes = lax.axis_size("sub")
    leaf_dev, rhs_count, points = charges.shape
    rank_size = basis.shape[1]
    group_size = coords.shape[0]
    clusters = far2_list.shape[0]
    group_boxes = transfer2.shape[0]
    start = lane * leaf_dev

    arrive = lax.dynamic_slice_in_dim(morton, start, leaf_dev, 0)
    slot = jnp.arange(group_size, dtype=jnp.int32)
    arrive_counts = jnp.sum(
        jnp.where(arrive[:, None] == slot[None, :], counts[None, :], 0), axis=1
    )
    point = jnp.arange(points, dtype=jnp.int32)
    block = jnp.where(
        point[None, None, :] < arrive_counts[:, None, None], charges, jnp.zeros((), charges.dtype)
    )
    blocks = gather_ring(block, "sub")
    mine = jnp.concatenate(blocks, axis=0)

    inverse = jnp.sum(jnp.where(morton[None, :] == slot[:, None], slot[None, :], 0), axis=1)
    place = lax.rem(inverse // leaf_dev - lane + lanes, lanes) * leaf_dev + inverse % leaf_dev
    places = jnp.concatenate(
        [
            slide(place, "leaf", 1),
            place + group_size,
            slide(place, "leaf", -1) + 2 * group_size,
            jnp.full((1,), 3 * group_size, jnp.int32),
        ]
    )
    wide = jnp.pad(coords.astype(jnp.float32), ((0, 0), (0, 1), (0, 0)))
    left_c = jnp.pad(slide(coords, "leaf", 1).astype(jnp.float32), ((0, 0), (0, 1), (0, 0)))
    right_c = jnp.pad(slide(coords, "leaf", -1).astype(jnp.float32), ((0, 0), (0, 1), (0, 0)))
    own_counts = lax.dynamic_slice_in_dim(counts, start, leaf_dev, 0)
    words, lists, bounds = plan_units(near_list, (group - 1) * group_size, group_size, own_counts)
    own_coords = lax.dynamic_slice_in_dim(wide, start, leaf_dev, 0)

    left_q = slide(mine, "leaf", 1)
    right_q = slide(mine, "leaf", -1)

    own_place = lax.dynamic_slice_in_dim(place, start, leaf_dev, 0)
    own_charges = mine[own_place]
    transfer_boxed = transfer1.reshape(clusters, 8, rank_size, rank_size)
    leaf_moments = jnp.einsum(
        "trp,tkp->trk", own_charges, basis, preferred_element_type=jnp.float32
    ).astype(jnp.bfloat16)
    box_moments = jnp.einsum(
        "bnrc,bncp->brp",
        leaf_moments.reshape(clusters, 8, rhs_count, rank_size),
        transfer_boxed,
        preferred_element_type=jnp.float32,
    ).astype(jnp.bfloat16)

    ring = jnp.stack(gather_ring(box_moments, "sub"))
    group_moments = jnp.roll(ring, lane, axis=0).reshape(group_boxes, rhs_count, rank_size)
    near_boxes = jnp.concatenate(
        [slide(group_moments, "leaf", 1), group_moments, slide(group_moments, "leaf", -1)], axis=0
    )
    top_moment = jnp.einsum(
        "brc,bcp->rp", group_moments, transfer2, preferred_element_type=jnp.float32
    ).astype(jnp.bfloat16)

    table = top_moment[None]
    reach = 1
    while reach < leaves:
        other = lax.ppermute(table, "leaf", [(i, i ^ reach) for i in range(leaves)])
        table = jnp.concatenate([table, other], axis=0)
        reach *= 2
    flipped = jnp.where(far3_list >= 0, far3_list ^ group, -1)
    top_field = far_field(table, flipped, coupling3, 0).astype(jnp.bfloat16)

    box_far = far_field(near_boxes, far2_list, coupling2, (group - 1) * group_boxes)
    own_transfer = lax.dynamic_slice_in_dim(transfer2, lane * clusters, clusters, 0)
    box_local = (
        box_far
        + jnp.einsum("rp,bcp->brc", top_field[0], own_transfer, preferred_element_type=jnp.float32)
    ).astype(jnp.bfloat16)
    leaf_local = jnp.einsum(
        "brp,bncp->bnrc", box_local, transfer_boxed, preferred_element_type=jnp.float32
    ).astype(jnp.bfloat16)
    leaf_local = leaf_local.reshape(leaf_dev, rhs_count, rank_size)
    far_part = jnp.einsum("trk,tkp->trp", leaf_local, basis, preferred_element_type=jnp.float32)

    near_part = near_field(
        words,
        lists,
        places,
        bounds,
        own_coords,
        (left_c, wide, right_c),
        (left_q, mine, right_q),
    )
    own_live = point[None, :] < own_counts[:, None]
    return jnp.where(own_live[:, None, :], near_part + far_part, jnp.zeros((), jnp.float32))


def solution(mesh):
    return jax.shard_map(
        on_device,
        mesh=mesh,
        in_specs=(
            P("leaf", None, None),
            P(("leaf", "sub"), None, None),
            P("leaf"),
            P("leaf"),
            P(("leaf", "sub"), None),
            P(("leaf", "sub"), None, None),
            P(("leaf", "sub"), None, None),
            P(("leaf", "sub"), None),
            P(("leaf", "sub"), None, None, None),
            P("leaf", None, None),
            P("leaf", None),
            P("leaf", None, None, None),
        ),
        out_specs=P(("leaf", "sub"), None, None),
        check_vma=False,
    )
```

```python
import functools

import jax
import jax.numpy as jnp
from jax import lax
from jax.experimental import pallas as pl
from jax.experimental.pallas import tpu as pltpu
from jax.sharding import PartitionSpec as P

kernel_scale = 0.07957747154594767
delta_squared = 0.0025

SLOTS = 4
UNITS = 16
STRIDE = 32
CLASSES = (128, 96, 64)
VMEM_LIMIT = 36 << 20


def shift(x, axis, by):
    count = lax.axis_size(axis)
    return lax.ppermute(x, axis, [(i, (i + by) % count) for i in range(count)])


def slide(x, axis, by):
    count = lax.axis_size(axis)
    pairs = [(i, i + by) for i in range(count) if 0 <= i + by < count]
    return lax.ppermute(x, axis, pairs)


def gather_ring(x, axis):
    count = lax.axis_size(axis)
    return [x] + [shift(x, axis, -k) for k in range(1, count)]


def prepare_targets(low, count, order, own_ref, tile_t):
    pick = lax.broadcasted_iota(jnp.int32, (8, 384), 1) // 128
    pick = (pick == lax.broadcasted_iota(jnp.int32, (8, 384), 0)).astype(jnp.bfloat16)
    targets = own_ref.shape[0]

    def body(w, _):
        for j in range(8):
            row = w * 8 + j
            own = own_ref[order[jnp.minimum(low + row, targets - 1)]]
            x = jnp.concatenate([own, jnp.zeros((4, 128), jnp.float32)], axis=0)
            wide = jnp.dot(x.T.astype(jnp.bfloat16), pick, preferred_element_type=jnp.float32)
            for c in range(3):
                tile_t[row * 3 + c] = wide[:, 128 * c : 128 * c + 128]
        return 0

    lax.fori_loop(0, (count + 7) // 8, body, 0)
    for c in range(3):
        tile_t[targets * 3 + c] = jnp.zeros((128, 128), jnp.float32)


def arrange_kernel(place, counts, b0, b1, b2, b3, out_ref, held, sems):
    rows = b0.shape[0]
    copies = [
        pltpu.make_async_copy(b, held.at[pl.ds(k * rows, rows)], sems.at[k])
        for k, b in enumerate((b0, b1, b2, b3))
    ]
    for copy in copies:
        copy.start()
    for copy in copies:
        copy.wait()
    point = lax.broadcasted_iota(jnp.int32, (8, 128), 1)

    def body(w, _):
        for j in range(16):
            s = w * 16 + j
            row = held[place[s]].astype(jnp.float32)
            out_ref[s] = jnp.where(point < counts[s], row, 0.0).astype(jnp.bfloat16)
        return 0

    lax.fori_loop(0, out_ref.shape[0] // 16, body, 0)


def arrange(place, counts, blocks):
    leaves = place.shape[0]
    whole = pl.BlockSpec(memory_space=pl.ANY)
    return pl.pallas_call(
        arrange_kernel,
        out_shape=jax.ShapeDtypeStruct((leaves, 8, 128), jnp.bfloat16),
        grid_spec=pltpu.PrefetchScalarGridSpec(
            num_scalar_prefetch=2,
            grid=(),
            in_specs=[whole] * 4,
            out_specs=pl.BlockSpec(memory_space=pltpu.VMEM),
            scratch_shapes=[
                pltpu.VMEM((leaves, 8, 128), jnp.bfloat16),
                pltpu.SemaphoreType.DMA((4,)),
            ],
        ),
        compiler_params=pltpu.CompilerParams(vmem_limit_bytes=8 << 20),
        cost_estimate=pl.CostEstimate(flops=1 << 20, bytes_accessed=2 << 20, transcendentals=0),
        name="arrange",
    )(place, counts, *blocks)


def near_steps(plan, low, high, own_ref, tile_t, src_c, src_q, acc, away):
    words, lists, bounds, ranks, order = plan
    bf = jnp.bfloat16
    targets = own_ref.shape[0]

    def rank_of(u):
        return ranks[lax.shift_right_logical(words[u], 5)]

    end = jnp.minimum(high * UNITS, bounds[4])
    some = end > low * UNITS
    base = jnp.where(some, rank_of(jnp.where(some, low * UNITS, 0)), 0)
    count = jnp.where(some, rank_of(jnp.where(some, end - 1, 0)) + 1 - base, 0)
    prepare_targets(base, count, order, own_ref, tile_t)

    def unit(word, rows):
        t = lax.shift_right_logical(word, 5)
        at = 3 * jnp.clip(ranks[t] - base, 0, targets)
        ids = [lists[word + k] - away for k in range(SLOTS)]
        charge = jnp.concatenate([src_q[i] for i in ids], axis=1)
        target = [
            [tile_t[at + c, 16 * m : 16 * m + 16, :].astype(bf) for c in range(3)]
            for m in range(rows // 16)
        ]
        columns = []
        for i in ids:
            source = [
                jnp.broadcast_to(src_c[i, c : c + 1, :], (16, 128)).astype(bf) for c in range(3)
            ]
            pieces = []
            for m in range(rows // 16):
                squared = None
                for c in range(3):
                    offset = target[m][c] - source[c]
                    if squared is None:
                        squared = offset * offset + jnp.asarray(delta_squared, bf)
                    else:
                        squared = squared + offset * offset
                pieces.append(lax.rsqrt(squared))
            columns.append(jnp.concatenate(pieces, axis=0))
        tile = jnp.concatenate(columns, axis=1)
        return t, lax.dot_general(
            charge, tile, (((1,), (1,)), ((), ())), preferred_element_type=jnp.float32
        )

    def step(rows, w, _):
        done = [unit(words[w * UNITS + j], rows) for j in range(UNITS)]
        for t, part in done:
            if rows < 128:
                part = jnp.concatenate([part, jnp.zeros((8, 128 - rows), jnp.float32)], axis=1)
            acc[t] = acc[t] + part * kernel_scale
        return 0

    for k, rows in enumerate(CLASSES):
        first = jnp.maximum(bounds[k], low)
        last = jnp.minimum(bounds[k + 1], high)
        lax.fori_loop(first, jnp.maximum(first, last), functools.partial(step, rows), 0)


def near_own_kernel(w, l, b, r, o, own_ref, c_ref, q_ref, acc, tile_t, src_c, src_q, sems):
    group = q_ref.shape[0]
    copies = [
        pltpu.make_async_copy(c_ref, src_c.at[pl.ds(0, group)], sems.at[0]),
        pltpu.make_async_copy(q_ref, src_q.at[pl.ds(0, group)], sems.at[1]),
    ]
    for copy in copies:
        copy.start()
    src_c[group] = jnp.zeros(src_c.shape[1:], src_c.dtype)
    src_q[group] = jnp.zeros(src_q.shape[1:], src_q.dtype)
    acc[...] = jnp.zeros_like(acc)
    for copy in copies:
        copy.wait()
    near_steps((w, l, b, r, o), 0, b[3], own_ref, tile_t, src_c, src_q, acc, group)


def near_first_kernel(
    share, w, l, b, r, o, own_ref, c0, c1, c2, q0, q1, q2, acc_in, acc, src_c, src_q, tile_t, sems
):
    group = q0.shape[0]
    copies = []
    for k, (c, q) in enumerate(((c0, q0), (c1, q1), (c2, q2))):
        rows = pl.ds(k * group, group)
        copies.append(pltpu.make_async_copy(c, src_c.at[rows], sems.at[k, 0]))
        copies.append(pltpu.make_async_copy(q, src_q.at[rows], sems.at[k, 1]))
    for copy in copies:
        copy.start()
    src_c[3 * group] = jnp.zeros(src_c.shape[1:], src_c.dtype)
    src_q[3 * group] = jnp.zeros(src_q.shape[1:], src_q.dtype)
    acc[...] = acc_in[...]
    for copy in copies:
        copy.wait()
    high = b[3] * share[1] // share[2]
    near_steps((w, l, b, r, o), 0, high, own_ref, tile_t, src_c, src_q, acc, 0)


def near_next_kernel(share, w, l, b, r, o, own_ref, src_c, src_q, acc_in, acc, tile_t):
    acc[...] = acc_in[...]
    low = b[3] * share[0] // share[2]
    high = b[3] * share[1] // share[2]
    near_steps((w, l, b, r, o), low, high, own_ref, tile_t, src_c, src_q, acc, 0)


near_params = pltpu.CompilerParams(vmem_limit_bytes=VMEM_LIMIT)
near_cost = pl.CostEstimate(flops=1 << 32, bytes_accessed=1 << 20, transcendentals=50 << 20)
in_vmem = pl.BlockSpec(memory_space=pltpu.VMEM)
in_place = pl.BlockSpec(memory_space=pl.ANY)


def tile_scratch(targets):
    return pltpu.VMEM((targets * 3 + 3, 128, 128), jnp.float32)


def near_own(plan, own_coords, coords, charges):
    group = charges.shape[0]
    targets = own_coords.shape[0]
    return pl.pallas_call(
        near_own_kernel,
        out_shape=jax.ShapeDtypeStruct((targets + 1, 8, 128), jnp.float32),
        grid_spec=pltpu.PrefetchScalarGridSpec(
            num_scalar_prefetch=5,
            grid=(),
            in_specs=[in_vmem] + [in_place] * 2,
            out_specs=in_vmem,
            scratch_shapes=[
                tile_scratch(targets),
                pltpu.VMEM((group + 1, 4, 128), jnp.float32),
                pltpu.VMEM((group + 1, 8, 128), jnp.bfloat16),
                pltpu.SemaphoreType.DMA((2,)),
            ],
        ),
        compiler_params=near_params,
        cost_estimate=near_cost,
        name="near_own",
    )(*plan, own_coords, coords, charges)


def near_first(share, plan, own_coords, coords, charges, acc):
    group = charges[0].shape[0]
    return pl.pallas_call(
        near_first_kernel,
        out_shape=(
            jax.ShapeDtypeStruct(acc.shape, jnp.float32),
            pltpu.VMEM((3 * group + 1, 4, 128), jnp.float32),
            pltpu.VMEM((3 * group + 1, 8, 128), jnp.bfloat16),
        ),
        grid_spec=pltpu.PrefetchScalarGridSpec(
            num_scalar_prefetch=6,
            grid=(),
            in_specs=[in_vmem] + [in_place] * 6 + [in_vmem],
            out_specs=(in_vmem,) * 3,
            scratch_shapes=[
                tile_scratch(own_coords.shape[0]),
                pltpu.SemaphoreType.DMA((3, 2)),
            ],
        ),
        compiler_params=near_params,
        cost_estimate=near_cost,
        name="near_first",
    )(share, *plan, own_coords, *coords, *charges, acc)


def near_next(share, plan, own_coords, src_c, src_q, acc):
    return pl.pallas_call(
        near_next_kernel,
        out_shape=jax.ShapeDtypeStruct(acc.shape, jnp.float32),
        grid_spec=pltpu.PrefetchScalarGridSpec(
            num_scalar_prefetch=6,
            grid=(),
            in_specs=[in_vmem] * 4,
            out_specs=in_vmem,
            scratch_shapes=[tile_scratch(own_coords.shape[0])],
        ),
        compiler_params=near_params,
        cost_estimate=near_cost,
        name="near_next",
    )(share, *plan, own_coords, src_c, src_q, acc)


def order_units(first, number, kind, targets, most):
    ids = jnp.arange(targets, dtype=jnp.int32)
    before = (kind[None, :] < kind[:, None]) | (
        (kind[None, :] == kind[:, None]) & (ids[None, :] < ids[:, None])
    )
    start = jnp.sum(jnp.where(before, number[None, :], 0), axis=1)
    classes = jnp.arange(len(CLASSES), dtype=jnp.int32)
    upto = jnp.sum(jnp.where(kind[None, :] <= classes[:, None], number[None, :], 0), axis=1)
    bounds = jnp.concatenate([jnp.zeros((1,), jnp.int32), (upto + UNITS - 1) // UNITS, upto[-1:]])
    unit = jnp.arange(most, dtype=jnp.int32)
    at = unit[:, None] - start[None, :]
    mine = (at >= 0) & (at < number[None, :])
    words = ids[None, :] * STRIDE + (first[None, :] + at) * SLOTS - targets * STRIDE
    return jnp.sum(jnp.where(mine, words, 0), axis=1) + targets * STRIDE, bounds


def plan_near(near_list, base, group, counts):
    targets, slots = near_list.shape
    dummy = 3 * group
    live = near_list >= 0
    local = jnp.where(live, jnp.clip(near_list - base, 0, dummy - 1), dummy)
    own = live & (local >= group) & (local < 2 * group)
    rest = live & ~own
    earlier = jnp.arange(slots)[:, None] < jnp.arange(slots)[None, :]
    own_number = jnp.sum(own, axis=1, dtype=jnp.int32)
    number = jnp.sum(live, axis=1, dtype=jnp.int32)
    own_rank = jnp.sum(own[:, :, None] & earlier[None], axis=1, dtype=jnp.int32)
    rest_rank = jnp.sum(rest[:, :, None] & earlier[None], axis=1, dtype=jnp.int32)
    rank = jnp.where(own, own_rank, jnp.where(rest, own_number[:, None] + rest_rank, STRIDE))
    slot = jnp.arange(STRIDE, dtype=jnp.int32)
    hit = rank[:, None, :] == slot[None, :, None]
    lists = jnp.sum(jnp.where(hit, local[:, None, :] - dummy, 0), axis=2) + dummy
    lists = jnp.pad(lists, ((0, 1), (0, 0)), constant_values=dummy).reshape(-1)
    kind = sum((counts <= rows).astype(jnp.int32) for rows in CLASSES[1:])
    whole = own_number // SLOTS
    units = (number + SLOTS - 1) // SLOTS
    most = targets * ((slots + SLOTS - 1) // SLOTS) + UNITS
    zero = jnp.zeros_like(whole)
    words_own, bounds_own = order_units(zero, whole, kind, targets, most)
    words_all, bounds_all = order_units(whole, units - whole, kind, targets, most)
    lists_own = jnp.where(lists == dummy, 2 * group, lists)
    ids = jnp.arange(targets, dtype=jnp.int32)
    before = (kind[None, :] < kind[:, None]) | (
        (kind[None, :] == kind[:, None]) & (ids[None, :] < ids[:, None])
    )
    ranks = jnp.sum(before, axis=1, dtype=jnp.int32)
    order = jnp.sum(jnp.where(ranks[None, :] == ids[:, None], ids[None, :], 0), axis=1)
    ranks = jnp.pad(ranks, (0, 1), constant_values=4 * targets)
    return (words_own, lists_own, bounds_own, ranks, order), (
        words_all,
        lists,
        bounds_all,
        ranks,
        order,
    )


def far_field(moments, lists, couplings, offset):
    valid = lists >= 0
    local = jnp.clip(lists - offset, 0, moments.shape[0] - 1)
    source = jnp.where(valid[..., None, None], moments[local], jnp.zeros((), moments.dtype))
    return jnp.einsum("bkrc,bkcp->brp", source, couplings, preferred_element_type=jnp.float32)


def on_device(
    coords,
    charges,
    counts,
    morton,
    near_list,
    basis,
    transfer1,
    far2_list,
    coupling2,
    transfer2,
    far3_list,
    coupling3,
):
    lane = lax.axis_index("sub")
    group = lax.axis_index("leaf")
    leaves = lax.axis_size("leaf")
    lanes = lax.axis_size("sub")
    leaf_dev, rhs_count, points = charges.shape
    rank_size = basis.shape[1]
    group_size = coords.shape[0]
    clusters = far2_list.shape[0]
    group_boxes = transfer2.shape[0]
    start = lane * leaf_dev

    tie = lax.optimization_barrier

    blocks = gather_ring(charges, "sub")
    own_counts = lax.dynamic_slice_in_dim(counts, start, leaf_dev, 0)
    wide = jnp.pad(coords.astype(jnp.float32), ((0, 0), (0, 1), (0, 0)))
    left_c = slide(wide, "leaf", 1)
    right_c = slide(wide, "leaf", -1)
    own_coords = lax.dynamic_slice_in_dim(wide, start, leaf_dev, 0)

    slot = jnp.arange(group_size, dtype=jnp.int32)
    inverse = jnp.sum(jnp.where(morton[None, :] == slot[:, None], slot[None, :], 0), axis=1)
    place = lax.rem(inverse // leaf_dev - lane + lanes, lanes) * leaf_dev + inverse % leaf_dev
    plan_own, plan_all = plan_near(near_list, (group - 1) * group_size, group_size, own_counts)

    blocks, left_c, right_c, plan_own, plan_all = tie((blocks, left_c, right_c, plan_own, plan_all))
    mine = arrange(place, counts, blocks)
    left_q = slide(mine, "leaf", 1)
    right_q = slide(mine, "leaf", -1)

    own_charges = lax.dynamic_slice_in_dim(mine, start, leaf_dev, 0)
    transfer_boxed = transfer1.reshape(clusters, 8, rank_size, rank_size)
    leaf_moments = jnp.einsum(
        "trp,tkp->trk", own_charges, basis, preferred_element_type=jnp.float32
    ).astype(jnp.bfloat16)
    box_moments = jnp.einsum(
        "bnrc,bncp->brp",
        leaf_moments.reshape(clusters, 8, rhs_count, rank_size),
        transfer_boxed,
        preferred_element_type=jnp.float32,
    ).astype(jnp.bfloat16)

    mine_after, box_moments = tie((mine, box_moments))
    ring = gather_ring(box_moments, "sub")
    acc = near_own(plan_own, own_coords, wide, mine_after)
    ring, acc = tie((ring, acc))
    group_moments = jnp.roll(jnp.stack(ring), lane, axis=0)
    group_moments = group_moments.reshape(group_boxes, rhs_count, rank_size)
    top_moment = jnp.einsum(
        "brc,bcp->rp", group_moments, transfer2, preferred_element_type=jnp.float32
    ).astype(jnp.bfloat16)

    table = top_moment[None]
    reach, rounds = 1, (leaves - 1).bit_length()
    for k in range(rounds):
        share = jnp.asarray([k, k + 1, rounds], jnp.int32)
        table, acc, group_moments = tie((table, acc, group_moments))
        other = lax.ppermute(table, "leaf", [(i, i ^ reach) for i in range(leaves)])
        if k == 0:
            acc, src_c, src_q = near_first(
                share, plan_all, own_coords, (left_c, wide, right_c), (left_q, mine, right_q), acc
            )
        else:
            acc = near_next(share, plan_all, own_coords, src_c, src_q, acc)
        if k == 1:
            left_b = slide(group_moments, "leaf", 1)
            right_b = slide(group_moments, "leaf", -1)
        if k == 3:
            table, left_b, right_b = tie((table, left_b, right_b))
        table = jnp.concatenate([table, other], axis=0)
        reach *= 2
    flipped = jnp.where(far3_list >= 0, far3_list ^ group, -1)
    top_field = far_field(table, flipped, coupling3, 0).astype(jnp.bfloat16)

    near_boxes = jnp.concatenate([left_b, group_moments, right_b], axis=0)
    box_far = far_field(near_boxes, far2_list, coupling2, (group - 1) * group_boxes)
    own_transfer = lax.dynamic_slice_in_dim(transfer2, lane * clusters, clusters, 0)
    box_local = (
        box_far
        + jnp.einsum("rp,bcp->brc", top_field[0], own_transfer, preferred_element_type=jnp.float32)
    ).astype(jnp.bfloat16)
    leaf_local = jnp.einsum(
        "brp,bncp->bnrc", box_local, transfer_boxed, preferred_element_type=jnp.float32
    ).astype(jnp.bfloat16)
    leaf_local = leaf_local.reshape(leaf_dev, rhs_count, rank_size)
    far_part = jnp.einsum("trk,tkp->trp", leaf_local, basis, preferred_element_type=jnp.float32)
    point = jnp.arange(points, dtype=jnp.int32)
    own_live = point[None, :] < own_counts[:, None]
    return jnp.where(own_live[:, None, :], acc[:leaf_dev] + far_part, jnp.zeros((), jnp.float32))


def solution(mesh):
    return jax.shard_map(
        on_device,
        mesh=mesh,
        in_specs=(
            P("leaf", None, None),
            P(("leaf", "sub"), None, None),
            P("leaf"),
            P("leaf"),
            P(("leaf", "sub"), None),
            P(("leaf", "sub"), None, None),
            P(("leaf", "sub"), None, None),
            P(("leaf", "sub"), None),
            P(("leaf", "sub"), None, None, None),
            P("leaf", None, None),
            P("leaf", None),
            P("leaf", None, None, None),
        ),
        out_specs=P(("leaf", "sub"), None, None),
        check_vma=False,
    )
```

```python
import functools

import jax
import jax.numpy as jnp
from jax import lax
from jax.experimental import pallas as pl
from jax.experimental.pallas import tpu as pltpu
from jax.sharding import PartitionSpec as P

kernel_scale = 0.07957747154594767
delta_squared = 0.0025

SLOTS = 4
UNITS = 16
STRIDE = 32
CLASSES = (128, 96, 64)
COSTS = (5, 4, 3)
OWN_UNITS = 2
VMEM_LIMIT = 36 << 20


def shift(x, axis, by):
    count = lax.axis_size(axis)
    return lax.ppermute(x, axis, [(i, (i + by) % count) for i in range(count)])


def slide(x, axis, by):
    count = lax.axis_size(axis)
    pairs = [(i, i + by) for i in range(count) if 0 <= i + by < count]
    return lax.ppermute(x, axis, pairs)


def gather_ring(x, axis):
    count = lax.axis_size(axis)
    return [x] + [shift(x, axis, -k) for k in range(1, count)]


def prepare_targets(low, count, order, first, src_c, tile_t):
    pick = lax.broadcasted_iota(jnp.int32, (8, 256), 1) // 128
    pick = (pick == lax.broadcasted_iota(jnp.int32, (8, 256), 0)).astype(jnp.bfloat16)
    line = lax.broadcasted_iota(jnp.int32, (8, 128), 0)
    targets = order.shape[0]

    def body(w, _):
        for j in range(8):
            row = w * 8 + j
            at = first + order[jnp.minimum(low + row, targets - 1)]
            x = [jnp.broadcast_to(src_c[c, pl.ds(at, 1), :], (8, 128)) for c in range(3)]
            x = jnp.where(line == 0, x[0], jnp.where(line == 1, x[1], x[2])).T
            wide = jnp.dot(x.astype(jnp.bfloat16), pick, preferred_element_type=jnp.float32)
            tile_t[row * 3] = wide[:, :128]
            tile_t[row * 3 + 1] = wide[:, 128:]
            tile_t[row * 3 + 2] = jnp.broadcast_to(x[:, 2:3], (128, 128))
        return 0

    lax.fori_loop(0, (count + 7) // 8, body, 0)
    for c in range(3):
        tile_t[targets * 3 + c] = jnp.zeros((128, 128), jnp.float32)


def arrange_kernel(place, counts, b0, b1, b2, b3, out_ref, held, sems):
    rows = b0.shape[0]
    copies = [
        pltpu.make_async_copy(b, held.at[pl.ds(k * rows, rows)], sems.at[k])
        for k, b in enumerate((b0, b1, b2, b3))
    ]
    for copy in copies:
        copy.start()
    for copy in copies:
        copy.wait()
    point = lax.broadcasted_iota(jnp.int32, (8, 128), 1)

    def body(w, _):
        for j in range(16):
            s = w * 16 + j
            row = held[place[s]].astype(jnp.float32)
            out_ref[s] = jnp.where(point < counts[s], row, 0.0).astype(jnp.bfloat16)
        return 0

    lax.fori_loop(0, out_ref.shape[0] // 16, body, 0)


def arrange(place, counts, blocks):
    leaves = place.shape[0]
    whole = pl.BlockSpec(memory_space=pl.ANY)
    return pl.pallas_call(
        arrange_kernel,
        out_shape=jax.ShapeDtypeStruct((leaves, 8, 128), jnp.bfloat16),
        grid_spec=pltpu.PrefetchScalarGridSpec(
            num_scalar_prefetch=2,
            grid=(),
            in_specs=[whole] * 4,
            out_specs=pl.BlockSpec(memory_space=pltpu.VMEM),
            scratch_shapes=[
                pltpu.VMEM((leaves, 8, 128), jnp.bfloat16),
                pltpu.SemaphoreType.DMA((4,)),
            ],
        ),
        compiler_params=pltpu.CompilerParams(vmem_limit_bytes=8 << 20),
        cost_estimate=pl.CostEstimate(flops=1 << 20, bytes_accessed=2 << 20, transcendentals=0),
        name="arrange",
    )(place, counts, *blocks)


def split(bounds, part, parts):
    left = jnp.int32(0)
    for k, cost in enumerate(COSTS):
        left = left + (bounds[k + 1] - bounds[k]) * cost
    left = left * part // parts
    at = jnp.int32(0)
    for k, cost in enumerate(COSTS):
        number = bounds[k + 1] - bounds[k]
        take = jnp.minimum(left // cost, number)
        at = at + take
        left = jnp.where(take == number, left - take * cost, 0)
    return at


def near_steps(plan, low, high, first_own, tile_t, src_c, src_q, acc, away):
    words, lists, bounds, ranks, order = plan
    bf = jnp.bfloat16
    targets = order.shape[0]

    def rank_of(u):
        return ranks[lax.shift_right_logical(words[u], 5)]

    end = jnp.minimum(high * UNITS, bounds[4])
    some = end > low * UNITS
    base = jnp.where(some, rank_of(jnp.where(some, low * UNITS, 0)), 0)
    count = jnp.where(some, rank_of(jnp.where(some, end - 1, 0)) + 1 - base, 0)
    prepare_targets(base, count, order, first_own, src_c, tile_t)

    def unit(word, rows):
        t = lax.shift_right_logical(word, 5)
        at = 3 * jnp.clip(ranks[t] - base, 0, targets)
        ids = [lists[word + k] - away for k in range(SLOTS)]
        charge = jnp.concatenate([src_q[i] for i in ids], axis=1)
        target = [
            [tile_t[at + c, 16 * m : 16 * m + 16, :].astype(bf) for c in range(3)]
            for m in range(rows // 16)
        ]
        columns = []
        for i in ids:
            source = [
                jnp.broadcast_to(src_c[c, pl.ds(i, 1), :], (16, 128)).astype(bf)
                for c in range(3)
            ]
            pieces = []
            for m in range(rows // 16):
                squared = None
                for c in range(3):
                    offset = target[m][c] - source[c]
                    if squared is None:
                        squared = offset * offset + jnp.asarray(delta_squared, bf)
                    else:
                        squared = squared + offset * offset
                pieces.append(lax.rsqrt(squared))
            columns.append(jnp.concatenate(pieces, axis=0))
        tile = jnp.concatenate(columns, axis=1)
        return t, lax.dot_general(
            charge, tile, (((1,), (1,)), ((), ())), preferred_element_type=jnp.float32
        )

    def step(rows, w, _):
        done = [unit(words[w * UNITS + j], rows) for j in range(UNITS)]
        for t, part in done:
            if rows < 128:
                part = jnp.concatenate([part, jnp.zeros((8, 128 - rows), jnp.float32)], axis=1)
            acc[t] = acc[t] + part * kernel_scale
        return 0

    for k, rows in enumerate(CLASSES):
        first = jnp.maximum(bounds[k], low)
        last = jnp.minimum(bounds[k + 1], high)
        lax.fori_loop(first, jnp.maximum(first, last), functools.partial(step, rows), 0)


def spread_coords(planes, src_c):
    group = planes[0].shape[1]
    for c in range(3):
        for k, plane in enumerate(planes):
            src_c[c, k * group : (k + 1) * group, :] = plane[c].astype(jnp.float32)
        src_c[c, len(planes) * group :, :] = jnp.zeros((8, 128), jnp.float32)


def near_own_kernel(share, w, l, b, r, o, c_ref, q_ref, acc, tile_t, src_c, src_q, sem):
    group = q_ref.shape[0]
    copy = pltpu.make_async_copy(q_ref, src_q.at[pl.ds(0, group)], sem)
    copy.start()
    src_q[group] = jnp.zeros(src_q.shape[1:], src_q.dtype)
    spread_coords([c_ref], src_c)
    acc[...] = jnp.zeros_like(acc)
    copy.wait()
    near_steps((w, l, b, r, o), 0, b[3], share[3], tile_t, src_c, src_q, acc, group)


def near_first_kernel(
    share, w, l, b, r, o, c0, c1, c2, q0, q1, q2, acc_in, acc, src_c, src_q, tile_t, sems
):
    group = q0.shape[0]
    copies = [
        pltpu.make_async_copy(q, src_q.at[pl.ds(k * group, group)], sems.at[k])
        for k, q in enumerate((q0, q1, q2))
    ]
    for copy in copies:
        copy.start()
    src_q[3 * group] = jnp.zeros(src_q.shape[1:], src_q.dtype)
    spread_coords([c0, c1, c2], src_c)
    acc[...] = acc_in[...]
    for copy in copies:
        copy.wait()
    high = split(b, share[1], share[2])
    near_steps((w, l, b, r, o), 0, high, group + share[3], tile_t, src_c, src_q, acc, 0)


def near_next_kernel(share, w, l, b, r, o, src_c, src_q, acc_in, acc, tile_t):
    group = src_q.shape[0] // 3
    acc[...] = acc_in[...]
    low = split(b, share[0], share[2])
    high = split(b, share[1], share[2])
    near_steps((w, l, b, r, o), low, high, group + share[3], tile_t, src_c, src_q, acc, 0)


near_params = pltpu.CompilerParams(vmem_limit_bytes=VMEM_LIMIT)
near_cost = pl.CostEstimate(flops=1 << 32, bytes_accessed=1 << 20, transcendentals=50 << 20)
in_vmem = pl.BlockSpec(memory_space=pltpu.VMEM)
in_place = pl.BlockSpec(memory_space=pl.ANY)


def tile_scratch(targets):
    return pltpu.VMEM((targets * 3 + 3, 128, 128), jnp.float32)


def near_own(share, plan, coords, charges, targets):
    group = charges.shape[0]
    return pl.pallas_call(
        near_own_kernel,
        out_shape=jax.ShapeDtypeStruct((targets + 1, 8, 128), jnp.float32),
        grid_spec=pltpu.PrefetchScalarGridSpec(
            num_scalar_prefetch=6,
            grid=(),
            in_specs=[in_vmem, in_place],
            out_specs=in_vmem,
            scratch_shapes=[
                tile_scratch(targets),
                pltpu.VMEM((3, group + 8, 128), jnp.float32),
                pltpu.VMEM((group + 1, 8, 128), jnp.bfloat16),
                pltpu.SemaphoreType.DMA,
            ],
        ),
        compiler_params=near_params,
        cost_estimate=near_cost,
        name="near_own",
    )(share, *plan, coords, charges)


def near_first(share, plan, coords, charges, acc):
    group = charges[0].shape[0]
    return pl.pallas_call(
        near_first_kernel,
        out_shape=(
            jax.ShapeDtypeStruct(acc.shape, jnp.float32),
            pltpu.VMEM((3, 3 * group + 8, 128), jnp.float32),
            pltpu.VMEM((3 * group + 1, 8, 128), jnp.bfloat16),
        ),
        grid_spec=pltpu.PrefetchScalarGridSpec(
            num_scalar_prefetch=6,
            grid=(),
            in_specs=[in_vmem] * 3 + [in_place] * 3 + [in_vmem],
            out_specs=(in_vmem,) * 3,
            scratch_shapes=[tile_scratch(acc.shape[0] - 1), pltpu.SemaphoreType.DMA((3,))],
        ),
        compiler_params=near_params,
        cost_estimate=near_cost,
        name="near_first",
    )(share, *plan, *coords, *charges, acc)


def near_next(share, plan, src_c, src_q, acc):
    return pl.pallas_call(
        near_next_kernel,
        out_shape=jax.ShapeDtypeStruct(acc.shape, jnp.float32),
        grid_spec=pltpu.PrefetchScalarGridSpec(
            num_scalar_prefetch=6,
            grid=(),
            in_specs=[in_vmem] * 3,
            out_specs=in_vmem,
            scratch_shapes=[tile_scratch(acc.shape[0] - 1)],
        ),
        compiler_params=near_params,
        cost_estimate=near_cost,
        name="near_next",
    )(share, *plan, src_c, src_q, acc)


def boxes_kernel(picks, left, mine, right, couple, out_ref, table):
    boxes, rhs, rank = out_ref.shape
    group = mine.shape[0]
    slots = picks.shape[0] // boxes
    for k, ref in enumerate((left, mine, right)):
        part = ref[...].astype(jnp.float32)
        table[k * group : (k + 1) * group] = jnp.concatenate([part, part], axis=2)
    table[3 * group] = jnp.zeros((rhs, 2 * rank), jnp.float32)
    low = lax.broadcasted_iota(jnp.int32, (rhs, 2 * rank), 1) < rank

    def body(w, _):
        for j in range(4):
            b = w * 4 + j
            total = jnp.zeros((rhs, rank), jnp.float32)
            for k in range(0, slots, 4):
                at = [table[picks[b * slots + k + i]] for i in range(4)]
                lhs = jnp.concatenate(
                    [jnp.where(low, at[0], at[1]), jnp.where(low, at[2], at[3])], axis=1
                )
                rhs_block = couple[pl.ds(b * slots + k, 4)].reshape(4 * rank, rank)
                total = total + jnp.dot(
                    lhs.astype(jnp.bfloat16), rhs_block, preferred_element_type=jnp.float32
                )
            out_ref[b] = total
        return 0

    lax.fori_loop(0, boxes // 4, body, 0)


def box_field(picks, left, mine, right, couple):
    boxes, slots, rank, _ = couple.shape
    rhs = mine.shape[1]
    return pl.pallas_call(
        boxes_kernel,
        out_shape=jax.ShapeDtypeStruct((boxes, rhs, rank), jnp.float32),
        grid_spec=pltpu.PrefetchScalarGridSpec(
            num_scalar_prefetch=1,
            grid=(),
            in_specs=[in_vmem] * 4,
            out_specs=in_vmem,
            scratch_shapes=[pltpu.VMEM((3 * mine.shape[0] + 1, rhs, 2 * rank), jnp.float32)],
        ),
        compiler_params=pltpu.CompilerParams(vmem_limit_bytes=12 << 20),
        cost_estimate=pl.CostEstimate(flops=1 << 24, bytes_accessed=4 << 20, transcendentals=0),
        name="box_field",
    )(picks, left, mine, right, couple.reshape(boxes * slots, rank, rank))


def down_kernel(flips, counts, share, table, c3, t2, box_far, t1, basis, near, out_ref, local):
    boxes, rhs, rank = box_far.shape
    leaves = out_ref.shape[0]
    bf = jnp.bfloat16
    across = (((1,), (1,)), ((), ()))
    top = jnp.zeros((rhs, rank), jnp.float32)
    for k in range(flips.shape[0]):
        at = flips[k]
        source = table[jnp.maximum(at, 0)].astype(jnp.float32)
        source = jnp.where(at >= 0, source, jnp.zeros_like(source)).astype(bf)
        top = top + jnp.dot(source, c3[k], preferred_element_type=jnp.float32)
    top = top.astype(bf)
    for b in range(boxes):
        part = lax.dot_general(top, t2[share[0] + b], across, preferred_element_type=jnp.float32)
        local[b] = (box_far[b] + part).astype(bf)
    point = lax.broadcasted_iota(jnp.int32, (rhs, 128), 1)
    fan = leaves // boxes

    def body(w, _):
        for j in range(2 * fan):
            t = w * 2 * fan + j
            moment = lax.dot_general(
                local[w * 2 + j // fan], t1[t], across, preferred_element_type=jnp.float32
            ).astype(bf)
            far = jnp.dot(moment, basis[t], preferred_element_type=jnp.float32)
            out_ref[t] = jnp.where(point < counts[t], near[t] + far, 0.0)
        return 0

    lax.fori_loop(0, boxes // 2, body, 0)


def go_down(flips, counts, share, table, c3, t2, box_far, t1, basis, near):
    leaves = counts.shape[0]
    return pl.pallas_call(
        down_kernel,
        out_shape=jax.ShapeDtypeStruct((leaves,) + near.shape[1:], jnp.float32),
        grid_spec=pltpu.PrefetchScalarGridSpec(
            num_scalar_prefetch=3,
            grid=(),
            in_specs=[in_vmem] * 7,
            out_specs=in_vmem,
            scratch_shapes=[pltpu.VMEM(box_far.shape, jnp.bfloat16)],
        ),
        compiler_params=pltpu.CompilerParams(vmem_limit_bytes=16 << 20),
        cost_estimate=pl.CostEstimate(flops=1 << 26, bytes_accessed=5 << 20, transcendentals=0),
        name="go_down",
    )(flips, counts, share, table, c3, t2, box_far, t1, basis, near)


def order_units(first, number, kind, targets, most):
    ids = jnp.arange(targets, dtype=jnp.int32)
    before = (kind[None, :] < kind[:, None]) | (
        (kind[None, :] == kind[:, None]) & (ids[None, :] < ids[:, None])
    )
    start = jnp.sum(jnp.where(before, number[None, :], 0), axis=1)
    classes = jnp.arange(len(CLASSES), dtype=jnp.int32)
    upto = jnp.sum(jnp.where(kind[None, :] <= classes[:, None], number[None, :], 0), axis=1)
    bounds = jnp.concatenate([jnp.zeros((1,), jnp.int32), (upto + UNITS - 1) // UNITS, upto[-1:]])
    unit = jnp.arange(most, dtype=jnp.int32)
    at = unit[:, None] - start[None, :]
    mine = (at >= 0) & (at < number[None, :])
    words = ids[None, :] * STRIDE + (first[None, :] + at) * SLOTS - targets * STRIDE
    return jnp.sum(jnp.where(mine, words, 0), axis=1) + targets * STRIDE, bounds


def plan_near(near_list, base, group, counts):
    targets, slots = near_list.shape
    dummy = 3 * group
    live = near_list >= 0
    local = jnp.where(live, jnp.clip(near_list - base, 0, dummy - 1), dummy)
    own = live & (local >= group) & (local < 2 * group)
    rest = live & ~own
    earlier = jnp.arange(slots)[:, None] < jnp.arange(slots)[None, :]
    own_number = jnp.sum(own, axis=1, dtype=jnp.int32)
    number = jnp.sum(live, axis=1, dtype=jnp.int32)
    own_rank = jnp.sum(own[:, :, None] & earlier[None], axis=1, dtype=jnp.int32)
    rest_rank = jnp.sum(rest[:, :, None] & earlier[None], axis=1, dtype=jnp.int32)
    rank = jnp.where(own, own_rank, jnp.where(rest, own_number[:, None] + rest_rank, STRIDE))
    slot = jnp.arange(STRIDE, dtype=jnp.int32)
    hit = rank[:, None, :] == slot[None, :, None]
    lists = jnp.sum(jnp.where(hit, local[:, None, :] - dummy, 0), axis=2) + dummy
    lists = jnp.pad(lists, ((0, 1), (0, 0)), constant_values=dummy).reshape(-1)
    kind = sum((counts <= rows).astype(jnp.int32) for rows in CLASSES[1:])
    whole = jnp.minimum(own_number // SLOTS, OWN_UNITS)
    units = (number + SLOTS - 1) // SLOTS
    most = targets * ((slots + SLOTS - 1) // SLOTS) + UNITS
    zero = jnp.zeros_like(whole)
    words_own, bounds_own = order_units(zero, whole, kind, targets, most)
    words_all, bounds_all = order_units(whole, units - whole, kind, targets, most)
    lists_own = jnp.where(lists == dummy, 2 * group, lists)
    ids = jnp.arange(targets, dtype=jnp.int32)
    before = (kind[None, :] < kind[:, None]) | (
        (kind[None, :] == kind[:, None]) & (ids[None, :] < ids[:, None])
    )
    ranks = jnp.sum(before, axis=1, dtype=jnp.int32)
    order = jnp.sum(jnp.where(ranks[None, :] == ids[:, None], ids[None, :], 0), axis=1)
    ranks = jnp.pad(ranks, (0, 1), constant_values=4 * targets)
    return (words_own, lists_own, bounds_own, ranks, order), (
        words_all,
        lists,
        bounds_all,
        ranks,
        order,
    )


def on_device(
    coords,
    charges,
    counts,
    morton,
    near_list,
    basis,
    transfer1,
    far2_list,
    coupling2,
    transfer2,
    far3_list,
    coupling3,
):
    lane = lax.axis_index("sub")
    group = lax.axis_index("leaf")
    leaves = lax.axis_size("leaf")
    lanes = lax.axis_size("sub")
    leaf_dev, rhs_count, points = charges.shape
    rank_size = basis.shape[1]
    group_size = coords.shape[0]
    clusters = far2_list.shape[0]
    group_boxes = transfer2.shape[0]
    start = lane * leaf_dev

    tie = lax.optimization_barrier

    blocks = gather_ring(charges, "sub")
    planes = jnp.transpose(coords, (1, 0, 2))
    left_c = slide(planes, "leaf", 1)
    right_c = slide(planes, "leaf", -1)
    own_counts = lax.dynamic_slice_in_dim(counts, start, leaf_dev, 0)

    slot = jnp.arange(group_size, dtype=jnp.int32)
    inverse = jnp.sum(jnp.where(morton[None, :] == slot[:, None], slot[None, :], 0), axis=1)
    place = lax.rem(inverse // leaf_dev - lane + lanes, lanes) * leaf_dev + inverse % leaf_dev
    plan_own, plan_all = plan_near(near_list, (group - 1) * group_size, group_size, own_counts)

    blocks, plan_own, plan_all = tie((blocks, plan_own, plan_all))
    mine = arrange(place, counts, blocks)
    mine, left_c, right_c = tie((mine, left_c, right_c))
    left_q = slide(mine, "leaf", 1)
    right_q = slide(mine, "leaf", -1)

    own_charges = lax.dynamic_slice_in_dim(mine, start, leaf_dev, 0)
    transfer_boxed = transfer1.reshape(clusters, 8, rank_size, rank_size)
    leaf_moments = jnp.einsum(
        "trp,tkp->trk", own_charges, basis, preferred_element_type=jnp.float32
    ).astype(jnp.bfloat16)
    box_moments = jnp.einsum(
        "bnrc,bncp->brp",
        leaf_moments.reshape(clusters, 8, rhs_count, rank_size),
        transfer_boxed,
        preferred_element_type=jnp.float32,
    ).astype(jnp.bfloat16)

    rounds = (leaves.bit_length() - 1) // 2

    def share_of(k):
        return jnp.stack([jnp.int32(k), jnp.int32(k + 1), jnp.int32(rounds), start])

    mine_after, box_moments = tie((mine, box_moments))
    ring = gather_ring(box_moments, "sub")
    acc = near_own(share_of(0), plan_own, planes, mine_after, leaf_dev)
    ring, acc = tie((ring, acc))
    group_moments = jnp.roll(jnp.stack(ring), lane, axis=0)
    group_moments = group_moments.reshape(group_boxes, rhs_count, rank_size)
    top_moment = jnp.einsum(
        "brc,bcp->rp", group_moments, transfer2, preferred_element_type=jnp.float32
    ).astype(jnp.bfloat16)

    far2_local = jnp.clip(far2_list - (group - 1) * group_boxes, 0, 3 * group_boxes - 1)
    picks = jnp.where(far2_list >= 0, far2_local, 3 * group_boxes).reshape(-1)
    table = top_moment[None]
    box_far = None
    for k in range(rounds):
        if k == rounds - 1:
            table, acc, box_far = tie((table, acc, box_far))
        else:
            table, acc = tie((table, acc))
        others = [
            lax.ppermute(table, "leaf", [(i, i ^ (m << 2 * k)) for i in range(leaves)])
            for m in (1, 2, 3)
        ]
        if k == 0:
            left_b = slide(group_moments, "leaf", 1)
            right_b = slide(group_moments, "leaf", -1)
            acc, src_c, src_q = near_first(
                share_of(k), plan_all, (left_c, planes, right_c), (left_q, mine, right_q), acc
            )
            others, left_b, right_b, acc = tie((others, left_b, right_b, acc))
        else:
            acc = near_next(share_of(k), plan_all, src_c, src_q, acc)
        if k == 1:
            box_far = box_field(picks, left_b, group_moments, right_b, coupling2)
        table = jnp.concatenate([table] + list(others), axis=0)
    flips = jnp.where(far3_list[0] >= 0, far3_list[0] ^ group, -1)
    lane_box = (lane * clusters)[None]
    return go_down(
        flips,
        own_counts,
        lane_box,
        table,
        coupling3[0],
        transfer2,
        box_far,
        transfer1,
        basis,
        acc,
    )


def solution(mesh):
    return jax.shard_map(
        on_device,
        mesh=mesh,
        in_specs=(
            P("leaf", None, None),
            P(("leaf", "sub"), None, None),
            P("leaf"),
            P("leaf"),
            P(("leaf", "sub"), None),
            P(("leaf", "sub"), None, None),
            P(("leaf", "sub"), None, None),
            P(("leaf", "sub"), None),
            P(("leaf", "sub"), None, None, None),
            P("leaf", None, None),
            P("leaf", None),
            P("leaf", None, None, None),
        ),
        out_specs=P(("leaf", "sub"), None, None),
        check_vma=False,
    )
```

```python
import functools

import jax
import jax.numpy as jnp
from jax import lax
from jax.experimental import pallas as pl
from jax.experimental.pallas import tpu as pltpu
from jax.sharding import PartitionSpec as P

kernel_scale = 0.07957747154594767
delta_squared = 0.0025

SLOTS = 4
UNITS = 16
STRIDE = 32
CLASSES = (128, 96, 64)
COSTS = (5, 4, 3)
OWN_UNITS = 2
VMEM_LIMIT = 33 << 20


LEAF = "leaf"
GATHER_ROWS = 16


def shift(x, axis, by):
    count = lax.axis_size(axis)
    return lax.ppermute(x, axis, [(i, (i + by) % count) for i in range(count)])


def slide(x, by):
    axis = LEAF
    count = lax.axis_size(axis)
    pairs = [(i, i + by) for i in range(count) if 0 <= i + by < count]
    return lax.ppermute(x, axis, pairs)


def gather_ring(x, axis):
    count = lax.axis_size(axis)
    return [x] + [shift(x, axis, -k) for k in range(1, count)]


def prepare_targets(low, count, order, first, src_c, tile_t):
    pick = lax.broadcasted_iota(jnp.int32, (8, 256), 1) // 128
    pick = (pick == lax.broadcasted_iota(jnp.int32, (8, 256), 0)).astype(jnp.bfloat16)
    line = lax.broadcasted_iota(jnp.int32, (8, 128), 0)
    targets = order.shape[0]

    def body(w, _):
        for j in range(8):
            row = w * 8 + j
            at = first + order[jnp.minimum(low + row, targets - 1)]
            x = [jnp.broadcast_to(src_c[c, pl.ds(at, 1), :], (8, 128)) for c in range(3)]
            x = jnp.where(line == 0, x[0], jnp.where(line == 1, x[1], x[2])).T
            wide = jnp.dot(x.astype(jnp.bfloat16), pick, preferred_element_type=jnp.float32)
            tile_t[row * 3] = wide[:, :128]
            tile_t[row * 3 + 1] = wide[:, 128:]
            tile_t[row * 3 + 2] = jnp.broadcast_to(x[:, 2:3], (128, 128))
        return 0

    lax.fori_loop(0, (count + 7) // 8, body, 0)
    for c in range(3):
        tile_t[targets * 3 + c] = jnp.zeros((128, 128), jnp.float32)


def arrange_kernel(place, counts, b0, b1, b2, b3, out_ref, held, sems):
    rows = b0.shape[0]
    copies = [
        pltpu.make_async_copy(b, held.at[pl.ds(k * rows, rows)], sems.at[k])
        for k, b in enumerate((b0, b1, b2, b3))
    ]
    for copy in copies:
        copy.start()
    for copy in copies:
        copy.wait()
    point = lax.broadcasted_iota(jnp.int32, (8, 128), 1)

    def body(w, _):
        for j in range(16):
            s = w * 16 + j
            row = held[place[s]].astype(jnp.float32)
            out_ref[s] = jnp.where(point < counts[s], row, 0.0).astype(jnp.bfloat16)
        return 0

    lax.fori_loop(0, out_ref.shape[0] // 16, body, 0)


def arrange(place, counts, blocks):
    leaves = place.shape[0]
    whole = pl.BlockSpec(memory_space=pl.ANY)
    return pl.pallas_call(
        arrange_kernel,
        out_shape=jax.ShapeDtypeStruct((leaves, 8, 128), jnp.bfloat16),
        grid_spec=pltpu.PrefetchScalarGridSpec(
            num_scalar_prefetch=2,
            grid=(),
            in_specs=[whole] * 4,
            out_specs=pl.BlockSpec(memory_space=pltpu.VMEM),
            scratch_shapes=[
                pltpu.VMEM((leaves, 8, 128), jnp.bfloat16),
                pltpu.SemaphoreType.DMA((4,)),
            ],
        ),
        compiler_params=pltpu.CompilerParams(vmem_limit_bytes=8 << 20),
        cost_estimate=pl.CostEstimate(flops=1 << 20, bytes_accessed=2 << 20, transcendentals=0),
        name="arrange",
    )(place, counts, *blocks)


def split(bounds, part, parts):
    left = jnp.int32(0)
    for k, cost in enumerate(COSTS):
        left = left + (bounds[k + 1] - bounds[k]) * cost
    left = left * part // parts
    at = jnp.int32(0)
    for k, cost in enumerate(COSTS):
        number = bounds[k + 1] - bounds[k]
        take = jnp.minimum(left // cost, number)
        at = at + take
        left = jnp.where(take == number, left - take * cost, 0)
    return at


def near_steps(plan, low, high, first_own, tile_t, src_c, src_q, acc, away):
    words, lists, bounds, ranks, order = plan
    bf = jnp.bfloat16
    targets = order.shape[0]

    def rank_of(u):
        return ranks[lax.shift_right_logical(words[u], 5)]

    end = jnp.minimum(high * UNITS, bounds[4])
    some = end > low * UNITS
    base = jnp.where(some, rank_of(jnp.where(some, low * UNITS, 0)), 0)
    count = jnp.where(some, rank_of(jnp.where(some, end - 1, 0)) + 1 - base, 0)
    prepare_targets(base, count, order, first_own, src_c, tile_t)

    def unit(word, rows):
        t = lax.shift_right_logical(word, 5)
        at = 3 * jnp.clip(ranks[t] - base, 0, targets)
        ids = [lists[word + k] - away for k in range(SLOTS)]
        charge = jnp.concatenate([src_q[i] for i in ids], axis=1)
        target = [
            [tile_t[at + c, 16 * m : 16 * m + 16, :].astype(bf) for c in range(3)]
            for m in range(rows // 16)
        ]
        columns = []
        for i in ids:
            source = [
                jnp.broadcast_to(src_c[c, pl.ds(i, 1), :], (16, 128)).astype(bf)
                for c in range(3)
            ]
            pieces = []
            for m in range(rows // 16):
                squared = None
                for c in range(3):
                    offset = target[m][c] - source[c]
                    if squared is None:
                        squared = offset * offset + jnp.asarray(delta_squared, bf)
                    else:
                        squared = squared + offset * offset
                pieces.append(lax.rsqrt(squared))
            columns.append(jnp.concatenate(pieces, axis=0))
        tile = jnp.concatenate(columns, axis=1)
        return t, lax.dot_general(
            charge, tile, (((1,), (1,)), ((), ())), preferred_element_type=jnp.float32
        )

    def step(rows, w, _):
        done = [unit(words[w * UNITS + j], rows) for j in range(UNITS)]
        for t, part in done:
            if rows < 128:
                part = jnp.concatenate([part, jnp.zeros((8, 128 - rows), jnp.float32)], axis=1)
            acc[t] = acc[t] + part * kernel_scale
        return 0

    for k, rows in enumerate(CLASSES):
        first = jnp.maximum(bounds[k], low)
        last = jnp.minimum(bounds[k + 1], high)
        lax.fori_loop(first, jnp.maximum(first, last), functools.partial(step, rows), 0)


def spread_coords(planes, src_c):
    group = planes[0].shape[1]
    for c in range(3):
        for k, plane in enumerate(planes):
            src_c[c, k * group : (k + 1) * group, :] = plane[c].astype(jnp.float32)
        src_c[c, len(planes) * group :, :] = jnp.zeros((8, 128), jnp.float32)


def near_own_kernel(share, w, l, b, r, o, c_ref, q_ref, acc, tile_t, src_c, src_q, sem):
    group = q_ref.shape[0]
    copy = pltpu.make_async_copy(q_ref, src_q.at[pl.ds(0, group)], sem)
    copy.start()
    src_q[group] = jnp.zeros(src_q.shape[1:], src_q.dtype)
    spread_coords([c_ref], src_c)
    acc[...] = jnp.zeros_like(acc)
    copy.wait()
    near_steps((w, l, b, r, o), 0, b[3], share[3], tile_t, src_c, src_q, acc, group)


def near_first_kernel(
    share, w, l, b, r, o, c0, c1, c2, q0, q1, q2, acc_in, acc, src_c, src_q, tile_t, sems
):
    group = q0.shape[0]
    copies = [
        pltpu.make_async_copy(q, src_q.at[pl.ds(k * group, group)], sems.at[k])
        for k, q in enumerate((q0, q1, q2))
    ]
    for copy in copies:
        copy.start()
    src_q[3 * group] = jnp.zeros(src_q.shape[1:], src_q.dtype)
    spread_coords([c0, c1, c2], src_c)
    acc[...] = acc_in[...]
    for copy in copies:
        copy.wait()
    high = split(b, share[1], share[2])
    near_steps((w, l, b, r, o), 0, high, group + share[3], tile_t, src_c, src_q, acc, 0)


def near_next_kernel(share, w, l, b, r, o, src_c, src_q, acc_in, acc, tile_t):
    group = src_q.shape[0] // 3
    acc[...] = acc_in[...]
    low = split(b, share[0], share[2])
    high = split(b, share[1], share[2])
    near_steps((w, l, b, r, o), low, high, group + share[3], tile_t, src_c, src_q, acc, 0)


near_params = pltpu.CompilerParams(vmem_limit_bytes=VMEM_LIMIT)
near_cost = pl.CostEstimate(flops=1 << 32, bytes_accessed=1 << 20, transcendentals=50 << 20)
in_vmem = pl.BlockSpec(memory_space=pltpu.VMEM)
in_place = pl.BlockSpec(memory_space=pl.ANY)


def tile_scratch(targets):
    return pltpu.VMEM((targets * 3 + 3, 128, 128), jnp.float32)


def near_own(share, plan, coords, charges, targets):
    group = charges.shape[0]
    return pl.pallas_call(
        near_own_kernel,
        out_shape=jax.ShapeDtypeStruct((targets + 1, 8, 128), jnp.float32),
        grid_spec=pltpu.PrefetchScalarGridSpec(
            num_scalar_prefetch=6,
            grid=(),
            in_specs=[in_vmem, in_place],
            out_specs=in_vmem,
            scratch_shapes=[
                tile_scratch(targets),
                pltpu.VMEM((3, group + 8, 128), jnp.float32),
                pltpu.VMEM((group + 1, 8, 128), jnp.bfloat16),
                pltpu.SemaphoreType.DMA,
            ],
        ),
        compiler_params=near_params,
        cost_estimate=near_cost,
        name="near_own",
    )(share, *plan, coords, charges)


def near_first(share, plan, coords, charges, acc):
    group = charges[0].shape[0]
    return pl.pallas_call(
        near_first_kernel,
        out_shape=(
            jax.ShapeDtypeStruct(acc.shape, jnp.float32),
            pltpu.VMEM((3, 3 * group + 8, 128), jnp.float32),
            pltpu.VMEM((3 * group + 1, 8, 128), jnp.bfloat16),
        ),
        grid_spec=pltpu.PrefetchScalarGridSpec(
            num_scalar_prefetch=6,
            grid=(),
            in_specs=[in_vmem] * 3 + [in_place] * 3 + [in_vmem],
            out_specs=(in_vmem,) * 3,
            scratch_shapes=[tile_scratch(acc.shape[0] - 1), pltpu.SemaphoreType.DMA((3,))],
        ),
        compiler_params=near_params,
        cost_estimate=near_cost,
        name="near_first",
    )(share, *plan, *coords, *charges, acc)


def near_next(share, plan, src_c, src_q, acc):
    return pl.pallas_call(
        near_next_kernel,
        out_shape=jax.ShapeDtypeStruct(acc.shape, jnp.float32),
        grid_spec=pltpu.PrefetchScalarGridSpec(
            num_scalar_prefetch=6,
            grid=(),
            in_specs=[in_vmem] * 3,
            out_specs=in_vmem,
            scratch_shapes=[tile_scratch(acc.shape[0] - 1)],
        ),
        compiler_params=near_params,
        cost_estimate=near_cost,
        name="near_next",
    )(share, *plan, src_c, src_q, acc)


def boxes_kernel(picks, left, mine, right, couple, out_ref, table):
    boxes, rhs, rank = out_ref.shape
    group = mine.shape[0]
    slots = picks.shape[0] // boxes
    for k, ref in enumerate((left, mine, right)):
        part = ref[...].astype(jnp.float32)
        table[k * group : (k + 1) * group] = jnp.concatenate([part, part], axis=2)
    table[3 * group] = jnp.zeros((rhs, 2 * rank), jnp.float32)
    low = lax.broadcasted_iota(jnp.int32, (rhs, 2 * rank), 1) < rank

    def body(w, _):
        for j in range(4):
            b = w * 4 + j
            total = jnp.zeros((rhs, rank), jnp.float32)
            for k in range(0, slots, 4):
                at = [table[picks[b * slots + k + i]] for i in range(4)]
                lhs = jnp.concatenate(
                    [jnp.where(low, at[0], at[1]), jnp.where(low, at[2], at[3])], axis=1
                )
                rhs_block = couple[pl.ds(b * slots + k, 4)].reshape(4 * rank, rank)
                total = total + jnp.dot(
                    lhs.astype(jnp.bfloat16), rhs_block, preferred_element_type=jnp.float32
                )
            out_ref[b] = total
        return 0

    lax.fori_loop(0, boxes // 4, body, 0)


def box_field(picks, left, mine, right, couple):
    boxes, slots, rank, _ = couple.shape
    rhs = mine.shape[1]
    return pl.pallas_call(
        boxes_kernel,
        out_shape=jax.ShapeDtypeStruct((boxes, rhs, rank), jnp.float32),
        grid_spec=pltpu.PrefetchScalarGridSpec(
            num_scalar_prefetch=1,
            grid=(),
            in_specs=[in_vmem] * 4,
            out_specs=in_vmem,
            scratch_shapes=[pltpu.VMEM((3 * mine.shape[0] + 1, rhs, 2 * rank), jnp.float32)],
        ),
        compiler_params=pltpu.CompilerParams(vmem_limit_bytes=12 << 20),
        cost_estimate=pl.CostEstimate(flops=1 << 24, bytes_accessed=4 << 20, transcendentals=0),
        name="box_field",
    )(picks, left, mine, right, couple.reshape(boxes * slots, rank, rank))


def down_kernel(flips, counts, share, table, c3, t2, box_far, t1, basis, near, out_ref, local):
    boxes, rhs, rank = box_far.shape
    leaves = out_ref.shape[0]
    bf = jnp.bfloat16
    across = (((1,), (1,)), ((), ()))
    top = jnp.zeros((rhs, rank), jnp.float32)
    for k in range(flips.shape[0]):
        at = flips[k]
        source = table[jnp.maximum(at, 0)].astype(jnp.float32)
        source = jnp.where(at >= 0, source, jnp.zeros_like(source)).astype(bf)
        top = top + jnp.dot(source, c3[k], preferred_element_type=jnp.float32)
    top = top.astype(bf)
    for b in range(boxes):
        part = lax.dot_general(top, t2[share[0] + b], across, preferred_element_type=jnp.float32)
        local[b] = (box_far[b] + part).astype(bf)
    point = lax.broadcasted_iota(jnp.int32, (rhs, 128), 1)
    fan = leaves // boxes

    def body(w, _):
        first = w * 2 * fan
        moments = [
            lax.dot_general(
                local[w * 2 + j // fan], t1[first + j], across, preferred_element_type=jnp.float32
            ).astype(bf)
            for j in range(2 * fan)
        ]
        fars = [
            jnp.dot(moments[j], basis[first + j], preferred_element_type=jnp.float32)
            for j in range(2 * fan)
        ]
        for j in range(2 * fan):
            t = first + j
            out_ref[t] = jnp.where(point < counts[t], near[t] + fars[j], 0.0)
        return 0

    lax.fori_loop(0, boxes // 2, body, 0)


def go_down(flips, counts, share, table, c3, t2, box_far, t1, basis, near):
    leaves = counts.shape[0]
    return pl.pallas_call(
        down_kernel,
        out_shape=jax.ShapeDtypeStruct((leaves,) + near.shape[1:], jnp.float32),
        grid_spec=pltpu.PrefetchScalarGridSpec(
            num_scalar_prefetch=3,
            grid=(),
            in_specs=[in_vmem] * 7,
            out_specs=in_vmem,
            scratch_shapes=[pltpu.VMEM(box_far.shape, jnp.bfloat16)],
        ),
        compiler_params=pltpu.CompilerParams(vmem_limit_bytes=16 << 20),
        cost_estimate=pl.CostEstimate(flops=1 << 26, bytes_accessed=5 << 20, transcendentals=0),
        name="go_down",
    )(flips, counts, share, table, c3, t2, box_far, t1, basis, near)


def order_units(first, number, kind, targets, most):
    ids = jnp.arange(targets, dtype=jnp.int32)
    before = (kind[None, :] < kind[:, None]) | (
        (kind[None, :] == kind[:, None]) & (ids[None, :] < ids[:, None])
    )
    start = jnp.sum(jnp.where(before, number[None, :], 0), axis=1)
    classes = jnp.arange(len(CLASSES), dtype=jnp.int32)
    upto = jnp.sum(jnp.where(kind[None, :] <= classes[:, None], number[None, :], 0), axis=1)
    bounds = jnp.concatenate([jnp.zeros((1,), jnp.int32), (upto + UNITS - 1) // UNITS, upto[-1:]])
    unit = jnp.arange(most, dtype=jnp.int32)
    at = unit[:, None] - start[None, :]
    mine = (at >= 0) & (at < number[None, :])
    words = ids[None, :] * STRIDE + (first[None, :] + at) * SLOTS - targets * STRIDE
    return jnp.sum(jnp.where(mine, words, 0), axis=1) + targets * STRIDE, bounds


def plan_near(near_list, base, group, counts):
    targets, slots = near_list.shape
    dummy = 3 * group
    live = near_list >= 0
    local = jnp.where(live, jnp.clip(near_list - base, 0, dummy - 1), dummy)
    own = live & (local >= group) & (local < 2 * group)
    rest = live & ~own
    earlier = jnp.arange(slots)[:, None] < jnp.arange(slots)[None, :]
    own_number = jnp.sum(own, axis=1, dtype=jnp.int32)
    number = jnp.sum(live, axis=1, dtype=jnp.int32)
    own_rank = jnp.sum(own[:, :, None] & earlier[None], axis=1, dtype=jnp.int32)
    rest_rank = jnp.sum(rest[:, :, None] & earlier[None], axis=1, dtype=jnp.int32)
    rank = jnp.where(own, own_rank, jnp.where(rest, own_number[:, None] + rest_rank, STRIDE))
    slot = jnp.arange(STRIDE, dtype=jnp.int32)
    hit = rank[:, None, :] == slot[None, :, None]
    lists = jnp.sum(jnp.where(hit, local[:, None, :] - dummy, 0), axis=2) + dummy
    lists = jnp.pad(lists, ((0, 1), (0, 0)), constant_values=dummy).reshape(-1)
    kind = sum((counts <= rows).astype(jnp.int32) for rows in CLASSES[1:])
    whole = jnp.minimum(own_number // SLOTS, OWN_UNITS)
    units = (number + SLOTS - 1) // SLOTS
    most = targets * ((slots + SLOTS - 1) // SLOTS) + UNITS
    zero = jnp.zeros_like(whole)
    words_own, bounds_own = order_units(zero, whole, kind, targets, most)
    words_all, bounds_all = order_units(whole, units - whole, kind, targets, most)
    lists_own = jnp.where(lists == dummy, 2 * group, lists)
    ids = jnp.arange(targets, dtype=jnp.int32)
    before = (kind[None, :] < kind[:, None]) | (
        (kind[None, :] == kind[:, None]) & (ids[None, :] < ids[:, None])
    )
    ranks = jnp.sum(before, axis=1, dtype=jnp.int32)
    order = jnp.sum(jnp.where(ranks[None, :] == ids[:, None], ids[None, :], 0), axis=1)
    ranks = jnp.pad(ranks, (0, 1), constant_values=4 * targets)
    return (words_own, lists_own, bounds_own, ranks, order), (
        words_all,
        lists,
        bounds_all,
        ranks,
        order,
    )


def on_device(
    coords,
    charges,
    counts,
    morton,
    near_list,
    basis,
    transfer1,
    far2_list,
    coupling2,
    transfer2,
    far3_list,
    coupling3,
):
    lane = lax.axis_index("sub")
    group = lax.axis_index(LEAF)
    lanes = lax.axis_size("sub")
    leaf_dev, rhs_count, points = charges.shape
    rank_size = basis.shape[1]
    group_size = coords.shape[0]
    clusters = far2_list.shape[0]
    group_boxes = transfer2.shape[0]
    start = lane * leaf_dev

    tie = lax.optimization_barrier

    blocks = gather_ring(charges, "sub")
    planes = jnp.transpose(coords, (1, 0, 2))
    left_c = slide(planes, 1)
    right_c = slide(planes, -1)
    own_counts = lax.dynamic_slice_in_dim(counts, start, leaf_dev, 0)

    slot = jnp.arange(group_size, dtype=jnp.int32)
    inverse = jnp.sum(jnp.where(morton[None, :] == slot[:, None], slot[None, :], 0), axis=1)
    place = lax.rem(inverse // leaf_dev - lane + lanes, lanes) * leaf_dev + inverse % leaf_dev
    plan_own, plan_all = plan_near(near_list, (group - 1) * group_size, group_size, own_counts)

    blocks, plan_own, plan_all = tie((blocks, plan_own, plan_all))
    mine = arrange(place, counts, blocks)
    mine, left_c, right_c = tie((mine, left_c, right_c))
    left_q = slide(mine, 1)
    right_q = slide(mine, -1)

    own_charges = lax.dynamic_slice_in_dim(mine, start, leaf_dev, 0)
    transfer_boxed = transfer1.reshape(clusters, 8, rank_size, rank_size)
    leaf_moments = jnp.einsum(
        "trp,tkp->trk", own_charges, basis, preferred_element_type=jnp.float32
    ).astype(jnp.bfloat16)
    box_moments = jnp.einsum(
        "bnrc,bncp->brp",
        leaf_moments.reshape(clusters, 8, rhs_count, rank_size),
        transfer_boxed,
        preferred_element_type=jnp.float32,
    ).astype(jnp.bfloat16)

    def share_of(low, high, parts):
        return jnp.stack([jnp.int32(low), jnp.int32(high), jnp.int32(parts), start])

    ring = gather_ring(box_moments, "sub")
    group_moments = jnp.roll(jnp.stack(ring), lane, axis=0)
    group_moments = group_moments.reshape(group_boxes, rhs_count, rank_size)
    top_moment = jnp.einsum(
        "brc,bcp->rp", group_moments, transfer2, preferred_element_type=jnp.float32
    ).astype(jnp.bfloat16)
    fill = ((0, GATHER_ROWS - 1), (0, 0), (0, 0))
    top_moment, mine_after = tie((jnp.pad(top_moment[None], fill), mine))
    table = lax.all_gather(top_moment, LEAF, axis=0, tiled=True)
    acc = near_own(share_of(0, 1, 1), plan_own, planes, mine_after, leaf_dev)
    group_moments, acc = tie((group_moments, acc))
    left_b = slide(group_moments, 1)
    right_b = slide(group_moments, -1)
    acc, src_c, src_q = near_first(
        share_of(0, 1, 1), plan_all, (left_c, planes, right_c), (left_q, mine, right_q), acc
    )
    far2_local = jnp.clip(far2_list - (group - 1) * group_boxes, 0, 3 * group_boxes - 1)
    picks = jnp.where(far2_list >= 0, far2_local, 3 * group_boxes).reshape(-1)
    left_b, acc = tie((left_b, acc))
    box_far = box_field(picks, left_b, group_moments, right_b, coupling2)
    flips = jnp.where(far3_list[0] >= 0, far3_list[0] * GATHER_ROWS, -1)
    lane_box = (lane * clusters)[None]
    return go_down(
        flips,
        own_counts,
        lane_box,
        table,
        coupling3[0],
        transfer2,
        box_far,
        transfer1,
        basis,
        acc,
    )


def solution(mesh):
    return jax.shard_map(
        on_device,
        mesh=mesh,
        in_specs=(
            P(LEAF, None, None),
            P((LEAF, "sub"), None, None),
            P(LEAF),
            P(LEAF),
            P((LEAF, "sub"), None),
            P((LEAF, "sub"), None, None),
            P((LEAF, "sub"), None, None),
            P((LEAF, "sub"), None),
            P((LEAF, "sub"), None, None, None),
            P(LEAF, None, None),
            P(LEAF, None),
            P(LEAF, None, None, None),
        ),
        out_specs=P((LEAF, "sub"), None, None),
        check_vma=False,
    )
```

```python
import functools

import jax
import jax.numpy as jnp
from jax import lax
from jax.experimental import pallas as pl
from jax.experimental.pallas import tpu as pltpu
from jax.sharding import PartitionSpec as P

kernel_scale = 0.07957747154594767
delta_squared = 0.0025

SLOTS = 4
UNITS = 16
STRIDE = 32
CLASSES = (128, 96, 64)
COSTS = (5, 4, 3)
OWN_UNITS = 2
VMEM_LIMIT = 36 << 20

in_vmem = pl.BlockSpec(memory_space=pltpu.VMEM)
in_place = pl.BlockSpec(memory_space=pl.ANY)


def shift(x, axis, by):
    count = lax.axis_size(axis)
    return lax.ppermute(x, axis, [(i, (i + by) % count) for i in range(count)])


def slide(x, axis, by):
    count = lax.axis_size(axis)
    pairs = [(i, i + by) for i in range(count) if 0 <= i + by < count]
    return lax.ppermute(x, axis, pairs)


def gather_ring(x, axis):
    count = lax.axis_size(axis)
    return [x] + [shift(x, axis, -k) for k in range(1, count)]


def prepare_targets(low, count, order, first, src_c, tile_t):
    pick = lax.broadcasted_iota(jnp.int32, (8, 256), 1) // 128
    pick = (pick == lax.broadcasted_iota(jnp.int32, (8, 256), 0)).astype(jnp.bfloat16)
    line = lax.broadcasted_iota(jnp.int32, (8, 128), 0)
    targets = order.shape[0]

    def body(w, _):
        for j in range(8):
            row = w * 8 + j
            at = first + order[jnp.minimum(low + row, targets - 1)]
            x = [jnp.broadcast_to(src_c[c, pl.ds(at, 1), :], (8, 128)) for c in range(3)]
            x = jnp.where(line == 0, x[0], jnp.where(line == 1, x[1], x[2])).T
            wide = jnp.dot(x.astype(jnp.bfloat16), pick, preferred_element_type=jnp.float32)
            tile_t[row * 3] = wide[:, :128]
            tile_t[row * 3 + 1] = wide[:, 128:]
            tile_t[row * 3 + 2] = jnp.broadcast_to(x[:, 2:3], (128, 128))
        return 0

    lax.fori_loop(0, (count + 7) // 8, body, 0)
    for c in range(3):
        tile_t[targets * 3 + c] = jnp.zeros((128, 128), jnp.float32)


def arrange_kernel(place, counts, b0, b1, b2, b3, coords, out_ref, held, sems):
    rows = b0.shape[0]
    leaves = place.shape[0]
    copies = [
        pltpu.make_async_copy(b, held.at[pl.ds(k * rows, rows)], sems.at[k])
        for k, b in enumerate((b0, b1, b2, b3))
    ]
    for copy in copies:
        copy.start()
    for copy in copies:
        copy.wait()
    point = lax.broadcasted_iota(jnp.int32, (8, 128), 1)

    def body(w, _):
        for j in range(16):
            s = w * 16 + j
            row = held[place[s]].astype(jnp.float32)
            out_ref[s] = jnp.where(point < counts[s], row, 0.0).astype(jnp.bfloat16)
        return 0

    out_ref[leaves:] = coords[...]
    lax.fori_loop(0, leaves // 16, body, 0)


def arrange(place, counts, blocks, planes):
    leaves = place.shape[0]
    coords = planes.reshape(-1, 8, 128)
    whole = pl.BlockSpec(memory_space=pl.ANY)
    return pl.pallas_call(
        arrange_kernel,
        out_shape=jax.ShapeDtypeStruct((leaves + coords.shape[0], 8, 128), jnp.bfloat16),
        grid_spec=pltpu.PrefetchScalarGridSpec(
            num_scalar_prefetch=2,
            grid=(),
            in_specs=[whole] * 4 + [in_vmem],
            out_specs=in_vmem,
            scratch_shapes=[
                pltpu.VMEM((leaves, 8, 128), jnp.bfloat16),
                pltpu.SemaphoreType.DMA((4,)),
            ],
        ),
        compiler_params=pltpu.CompilerParams(vmem_limit_bytes=8 << 20),
        cost_estimate=pl.CostEstimate(flops=1 << 20, bytes_accessed=2 << 20, transcendentals=0),
        name="arrange",
    )(place, counts, *blocks, coords)


def split(bounds, part, parts):
    left = jnp.int32(0)
    for k, cost in enumerate(COSTS):
        left = left + (bounds[k + 1] - bounds[k]) * cost
    left = left * part // parts
    at = jnp.int32(0)
    for k, cost in enumerate(COSTS):
        number = bounds[k + 1] - bounds[k]
        take = jnp.minimum(left // cost, number)
        at = at + take
        left = jnp.where(take == number, left - take * cost, 0)
    return at


def near_steps(plan, low, high, first_own, tile_t, src_c, src_q, acc, away):
    words, lists, bounds, ranks, order = plan
    bf = jnp.bfloat16
    targets = order.shape[0]

    def rank_of(u):
        return ranks[lax.shift_right_logical(words[u], 5)]

    end = jnp.minimum(high * UNITS, bounds[4])
    some = end > low * UNITS
    base = jnp.where(some, rank_of(jnp.where(some, low * UNITS, 0)), 0)
    count = jnp.where(some, rank_of(jnp.where(some, end - 1, 0)) + 1 - base, 0)
    prepare_targets(base, count, order, first_own, src_c, tile_t)

    def unit(word, rows):
        t = lax.shift_right_logical(word, 5)
        at = 3 * jnp.clip(ranks[t] - base, 0, targets)
        ids = [lists[word + k] - away for k in range(SLOTS)]
        charge = jnp.concatenate([src_q[i] for i in ids], axis=1)
        target = [
            [tile_t[at + c, 16 * m : 16 * m + 16, :].astype(bf) for c in range(3)]
            for m in range(rows // 16)
        ]
        columns = []
        for i in ids:
            source = [
                jnp.broadcast_to(src_c[c, pl.ds(i, 1), :], (16, 128)).astype(bf)
                for c in range(3)
            ]
            pieces = []
            for m in range(rows // 16):
                squared = None
                for c in range(3):
                    offset = target[m][c] - source[c]
                    if squared is None:
                        squared = offset * offset + jnp.asarray(delta_squared, bf)
                    else:
                        squared = squared + offset * offset
                pieces.append(lax.rsqrt(squared))
            columns.append(jnp.concatenate(pieces, axis=0))
        tile = jnp.concatenate(columns, axis=1)
        return t, lax.dot_general(
            charge, tile, (((1,), (1,)), ((), ())), preferred_element_type=jnp.float32
        )

    def step(rows, w, _):
        done = [unit(words[w * UNITS + j], rows) for j in range(UNITS)]
        for t, part in done:
            if rows < 128:
                part = jnp.concatenate([part, jnp.zeros((8, 128 - rows), jnp.float32)], axis=1)
            acc[t] = acc[t] + part * kernel_scale
        return 0

    for k, rows in enumerate(CLASSES):
        first = jnp.maximum(bounds[k], low)
        last = jnp.minimum(bounds[k + 1], high)
        lax.fori_loop(first, jnp.maximum(first, last), functools.partial(step, rows), 0)


def near_own_kernel(share, w, l, b, r, o, c_ref, q_ref, acc, tile_t, src_c, src_q, sem):
    group = c_ref.shape[1]
    copy = pltpu.make_async_copy(q_ref.at[pl.ds(0, group)], src_q.at[pl.ds(0, group)], sem)
    copy.start()
    src_q[group] = jnp.zeros(src_q.shape[1:], src_q.dtype)
    for c in range(3):
        src_c[c, :group, :] = c_ref[c].astype(jnp.float32)
        src_c[c, group:, :] = jnp.zeros((8, 128), jnp.float32)
    acc[...] = jnp.zeros_like(acc)
    copy.wait()
    near_steps((w, l, b, r, o), 0, b[3], share[3], tile_t, src_c, src_q, acc, group)


def near_first_kernel(
    share, w, l, b, r, o, x0, x1, x2, acc_in, acc, src_c, src_q, tile_t, stage, sems
):
    packs = (x0, x1, x2)
    eights = stage.shape[1]
    group = x0.shape[0] - eights
    copies = [
        pltpu.make_async_copy(x.at[pl.ds(group, eights)], stage.at[k], sems.at[k, 0])
        for k, x in enumerate(packs)
    ] + [
        pltpu.make_async_copy(
            x.at[pl.ds(0, group)], src_q.at[pl.ds(k * group, group)], sems.at[k, 1]
        )
        for k, x in enumerate(packs)
    ]
    for copy in copies:
        copy.start()
    src_q[3 * group] = jnp.zeros(src_q.shape[1:], src_q.dtype)
    acc[...] = acc_in[...]
    for copy in copies[:3]:
        copy.wait()
    for c in range(3):
        src_c[c, 3 * group :, :] = jnp.zeros((8, 128), jnp.float32)

        def spread(w, _):
            for k in range(3):
                for j in range(4):
                    i = w * 4 + j
                    rows = pl.ds(pl.multiple_of(k * group + 8 * i, 8), 8)
                    src_c[c, rows, :] = stage[k, c * (group // 8) + i].astype(jnp.float32)
            return 0

        lax.fori_loop(0, group // 32, spread, 0)
    for copy in copies[3:]:
        copy.wait()
    high = split(b, share[1], share[2])
    near_steps((w, l, b, r, o), 0, high, group + share[3], tile_t, src_c, src_q, acc, 0)


def near_next_kernel(share, w, l, b, r, o, src_c, src_q, acc_in, acc, tile_t):
    group = src_q.shape[0] // 3
    acc[...] = acc_in[...]
    low = split(b, share[0], share[2])
    high = split(b, share[1], share[2])
    near_steps((w, l, b, r, o), low, high, group + share[3], tile_t, src_c, src_q, acc, 0)


near_params = pltpu.CompilerParams(vmem_limit_bytes=VMEM_LIMIT)
near_cost = pl.CostEstimate(flops=1 << 32, bytes_accessed=1 << 20, transcendentals=50 << 20)


def tile_scratch(targets):
    return pltpu.VMEM((targets * 3 + 3, 128, 128), jnp.float32)


def near_own(share, plan, coords, charges, targets):
    group = coords.shape[1]
    return pl.pallas_call(
        near_own_kernel,
        out_shape=jax.ShapeDtypeStruct((targets + 1, 8, 128), jnp.float32),
        grid_spec=pltpu.PrefetchScalarGridSpec(
            num_scalar_prefetch=6,
            grid=(),
            in_specs=[in_vmem, in_place],
            out_specs=in_vmem,
            scratch_shapes=[
                tile_scratch(targets),
                pltpu.VMEM((3, group + 8, 128), jnp.float32),
                pltpu.VMEM((group + 1, 8, 128), jnp.bfloat16),
                pltpu.SemaphoreType.DMA,
            ],
        ),
        compiler_params=near_params,
        cost_estimate=near_cost,
        name="near_own",
    )(share, *plan, coords, charges)


def near_first(share, plan, packs, acc, group):
    return pl.pallas_call(
        near_first_kernel,
        out_shape=(
            jax.ShapeDtypeStruct(acc.shape, jnp.float32),
            pltpu.VMEM((3, 3 * group + 8, 128), jnp.float32),
            pltpu.VMEM((3 * group + 1, 8, 128), jnp.bfloat16),
        ),
        grid_spec=pltpu.PrefetchScalarGridSpec(
            num_scalar_prefetch=6,
            grid=(),
            in_specs=[in_place] * 3 + [in_vmem],
            out_specs=(in_vmem,) * 3,
            scratch_shapes=[
                tile_scratch(acc.shape[0] - 1),
                pltpu.VMEM((3, packs[0].shape[0] - group, 8, 128), jnp.bfloat16),
                pltpu.SemaphoreType.DMA((3, 2)),
            ],
        ),
        compiler_params=near_params,
        cost_estimate=near_cost,
        name="near_first",
    )(share, *plan, *packs, acc)


def near_next(share, plan, src_c, src_q, acc):
    return pl.pallas_call(
        near_next_kernel,
        out_shape=jax.ShapeDtypeStruct(acc.shape, jnp.float32),
        grid_spec=pltpu.PrefetchScalarGridSpec(
            num_scalar_prefetch=6,
            grid=(),
            in_specs=[in_vmem] * 3,
            out_specs=in_vmem,
            scratch_shapes=[tile_scratch(acc.shape[0] - 1)],
        ),
        compiler_params=near_params,
        cost_estimate=near_cost,
        name="near_next",
    )(share, *plan, src_c, src_q, acc)


def boxes_kernel(picks, left, mine, right, couple, out_ref, table):
    boxes, rhs, rank = out_ref.shape
    group = mine.shape[0]
    slots = picks.shape[0] // boxes
    for k, ref in enumerate((left, mine, right)):
        part = ref[...].astype(jnp.float32)
        table[k * group : (k + 1) * group] = jnp.concatenate([part, part], axis=2)
    table[3 * group] = jnp.zeros((rhs, 2 * rank), jnp.float32)
    low = lax.broadcasted_iota(jnp.int32, (rhs, 2 * rank), 1) < rank

    def body(w, _):
        for j in range(4):
            b = w * 4 + j
            total = jnp.zeros((rhs, rank), jnp.float32)
            for k in range(0, slots, 4):
                at = [table[picks[b * slots + k + i]] for i in range(4)]
                lhs = jnp.concatenate(
                    [jnp.where(low, at[0], at[1]), jnp.where(low, at[2], at[3])], axis=1
                )
                rhs_block = couple[pl.ds(b * slots + k, 4)].reshape(4 * rank, rank)
                total = total + jnp.dot(
                    lhs.astype(jnp.bfloat16), rhs_block, preferred_element_type=jnp.float32
                )
            out_ref[b] = total
        return 0

    lax.fori_loop(0, boxes // 4, body, 0)


def box_field(picks, left, mine, right, couple):
    boxes, slots, rank, _ = couple.shape
    rhs = mine.shape[1]
    return pl.pallas_call(
        boxes_kernel,
        out_shape=jax.ShapeDtypeStruct((boxes, rhs, rank), jnp.float32),
        grid_spec=pltpu.PrefetchScalarGridSpec(
            num_scalar_prefetch=1,
            grid=(),
            in_specs=[in_vmem] * 4,
            out_specs=in_vmem,
            scratch_shapes=[pltpu.VMEM((3 * mine.shape[0] + 1, rhs, 2 * rank), jnp.float32)],
        ),
        compiler_params=pltpu.CompilerParams(vmem_limit_bytes=12 << 20),
        cost_estimate=pl.CostEstimate(flops=1 << 24, bytes_accessed=4 << 20, transcendentals=0),
        name="box_field",
    )(picks, left, mine, right, couple.reshape(boxes * slots, rank, rank))


def down_kernel(flips, counts, share, table, c3, t2, box_far, t1, basis, near, out_ref, local):
    boxes, rhs, rank = box_far.shape
    leaves = out_ref.shape[0]
    bf = jnp.bfloat16
    across = (((1,), (1,)), ((), ()))
    top = jnp.zeros((rhs, rank), jnp.float32)
    for k in range(flips.shape[0]):
        at = flips[k]
        source = table[jnp.maximum(at, 0)].astype(jnp.float32)
        source = jnp.where(at >= 0, source, jnp.zeros_like(source)).astype(bf)
        top = top + jnp.dot(source, c3[k], preferred_element_type=jnp.float32)
    top = top.astype(bf)
    for b in range(boxes):
        part = lax.dot_general(top, t2[share[0] + b], across, preferred_element_type=jnp.float32)
        local[b] = (box_far[b] + part).astype(bf)
    point = lax.broadcasted_iota(jnp.int32, (rhs, 128), 1)
    fan = leaves // boxes

    def body(w, _):
        first = w * 2 * fan
        moments = [
            lax.dot_general(
                local[w * 2 + j // fan], t1[first + j], across, preferred_element_type=jnp.float32
            ).astype(bf)
            for j in range(2 * fan)
        ]
        fars = [
            jnp.dot(moments[j], basis[first + j], preferred_element_type=jnp.float32)
            for j in range(2 * fan)
        ]
        for j in range(2 * fan):
            t = first + j
            out_ref[t] = jnp.where(point < counts[t], near[t] + fars[j], 0.0)
        return 0

    lax.fori_loop(0, boxes // 2, body, 0)


def go_down(flips, counts, share, table, c3, t2, box_far, t1, basis, near):
    leaves = counts.shape[0]
    return pl.pallas_call(
        down_kernel,
        out_shape=jax.ShapeDtypeStruct((leaves,) + near.shape[1:], jnp.float32),
        grid_spec=pltpu.PrefetchScalarGridSpec(
            num_scalar_prefetch=3,
            grid=(),
            in_specs=[in_vmem] * 7,
            out_specs=in_vmem,
            scratch_shapes=[pltpu.VMEM(box_far.shape, jnp.bfloat16)],
        ),
        compiler_params=pltpu.CompilerParams(vmem_limit_bytes=16 << 20),
        cost_estimate=pl.CostEstimate(flops=1 << 26, bytes_accessed=5 << 20, transcendentals=0),
        name="go_down",
    )(flips, counts, share, table, c3, t2, box_far, t1, basis, near)


def order_units(first, number, kind, targets, most):
    ids = jnp.arange(targets, dtype=jnp.int32)
    before = (kind[None, :] < kind[:, None]) | (
        (kind[None, :] == kind[:, None]) & (ids[None, :] < ids[:, None])
    )
    start = jnp.sum(jnp.where(before, number[None, :], 0), axis=1)
    classes = jnp.arange(len(CLASSES), dtype=jnp.int32)
    upto = jnp.sum(jnp.where(kind[None, :] <= classes[:, None], number[None, :], 0), axis=1)
    bounds = jnp.concatenate([jnp.zeros((1,), jnp.int32), (upto + UNITS - 1) // UNITS, upto[-1:]])
    unit = jnp.arange(most, dtype=jnp.int32)
    at = unit[:, None] - start[None, :]
    mine = (at >= 0) & (at < number[None, :])
    words = ids[None, :] * STRIDE + (first[None, :] + at) * SLOTS - targets * STRIDE
    return jnp.sum(jnp.where(mine, words, 0), axis=1) + targets * STRIDE, bounds


def plan_near(near_list, base, group, counts):
    targets, slots = near_list.shape
    dummy = 3 * group
    live = near_list >= 0
    local = jnp.where(live, jnp.clip(near_list - base, 0, dummy - 1), dummy)
    own = live & (local >= group) & (local < 2 * group)
    rest = live & ~own
    earlier = jnp.arange(slots)[:, None] < jnp.arange(slots)[None, :]
    own_number = jnp.sum(own, axis=1, dtype=jnp.int32)
    number = jnp.sum(live, axis=1, dtype=jnp.int32)
    own_rank = jnp.sum(own[:, :, None] & earlier[None], axis=1, dtype=jnp.int32)
    rest_rank = jnp.sum(rest[:, :, None] & earlier[None], axis=1, dtype=jnp.int32)
    rank = jnp.where(own, own_rank, jnp.where(rest, own_number[:, None] + rest_rank, STRIDE))
    slot = jnp.arange(STRIDE, dtype=jnp.int32)
    hit = rank[:, None, :] == slot[None, :, None]
    lists = jnp.sum(jnp.where(hit, local[:, None, :] - dummy, 0), axis=2) + dummy
    lists = jnp.pad(lists, ((0, 1), (0, 0)), constant_values=dummy).reshape(-1)
    kind = sum((counts <= rows).astype(jnp.int32) for rows in CLASSES[1:])
    whole = jnp.minimum(own_number // SLOTS, OWN_UNITS)
    units = (number + SLOTS - 1) // SLOTS
    most = targets * ((slots + SLOTS - 1) // SLOTS) + UNITS
    zero = jnp.zeros_like(whole)
    words_own, bounds_own = order_units(zero, whole, kind, targets, most)
    words_all, bounds_all = order_units(whole, units - whole, kind, targets, most)
    lists_own = jnp.where(lists == dummy, 2 * group, lists)
    ids = jnp.arange(targets, dtype=jnp.int32)
    before = (kind[None, :] < kind[:, None]) | (
        (kind[None, :] == kind[:, None]) & (ids[None, :] < ids[:, None])
    )
    ranks = jnp.sum(before, axis=1, dtype=jnp.int32)
    order = jnp.sum(jnp.where(ranks[None, :] == ids[:, None], ids[None, :], 0), axis=1)
    ranks = jnp.pad(ranks, (0, 1), constant_values=4 * targets)
    return (words_own, lists_own, bounds_own, ranks, order), (
        words_all,
        lists,
        bounds_all,
        ranks,
        order,
    )


def on_device(
    coords,
    charges,
    counts,
    morton,
    near_list,
    basis,
    transfer1,
    far2_list,
    coupling2,
    transfer2,
    far3_list,
    coupling3,
):
    lane = lax.axis_index("sub")
    group = lax.axis_index("leaf")
    leaves = lax.axis_size("leaf")
    lanes = lax.axis_size("sub")
    leaf_dev, rhs_count, points = charges.shape
    rank_size = basis.shape[1]
    group_size = coords.shape[0]
    clusters = far2_list.shape[0]
    group_boxes = transfer2.shape[0]
    start = lane * leaf_dev

    tie = lax.optimization_barrier

    blocks = gather_ring(charges, "sub")
    planes = jnp.transpose(coords, (1, 0, 2))
    own_counts = lax.dynamic_slice_in_dim(counts, start, leaf_dev, 0)

    slot = jnp.arange(group_size, dtype=jnp.int32)
    inverse = jnp.sum(jnp.where(morton[None, :] == slot[:, None], slot[None, :], 0), axis=1)
    place = lax.rem(inverse // leaf_dev - lane + lanes, lanes) * leaf_dev + inverse % leaf_dev
    plan_own, plan_all = plan_near(near_list, (group - 1) * group_size, group_size, own_counts)

    blocks, plan_own, plan_all = tie((blocks, plan_own, plan_all))
    mine = arrange(place, counts, blocks, planes)
    left = slide(mine, "leaf", 1)
    right = slide(mine, "leaf", -1)

    own_charges = lax.dynamic_slice_in_dim(mine, start, leaf_dev, 0)
    transfer_boxed = transfer1.reshape(clusters, 8, rank_size, rank_size)
    leaf_moments = jnp.einsum(
        "trp,tkp->trk", own_charges, basis, preferred_element_type=jnp.float32
    ).astype(jnp.bfloat16)
    box_moments = jnp.einsum(
        "bnrc,bncp->brp",
        leaf_moments.reshape(clusters, 8, rhs_count, rank_size),
        transfer_boxed,
        preferred_element_type=jnp.float32,
    ).astype(jnp.bfloat16)

    rounds = (leaves.bit_length() - 1) // 2

    def share_of(k):
        return jnp.stack([jnp.int32(k), jnp.int32(k + 1), jnp.int32(rounds), start])

    mine_after, box_moments = tie((mine, box_moments))
    ring = gather_ring(box_moments, "sub")
    acc = near_own(share_of(0), plan_own, planes, mine_after, leaf_dev)
    ring, acc = tie((ring, acc))
    group_moments = jnp.roll(jnp.stack(ring), lane, axis=0)
    group_moments = group_moments.reshape(group_boxes, rhs_count, rank_size)
    top_moment = jnp.einsum(
        "brc,bcp->rp", group_moments, transfer2, preferred_element_type=jnp.float32
    ).astype(jnp.bfloat16)

    far2_local = jnp.clip(far2_list - (group - 1) * group_boxes, 0, 3 * group_boxes - 1)
    odd = lax.rem(group, 2) == 1
    block = far2_local // group_boxes
    block = jnp.where(odd, 2 - block, block)
    far2_local = block * group_boxes + far2_local % group_boxes
    picks = jnp.where(far2_list >= 0, far2_local, 3 * group_boxes).reshape(-1)
    table = top_moment[None]
    box_far = None
    for k in range(rounds):
        if k == rounds - 1:
            table, acc, box_far = tie((table, acc, box_far))
        else:
            table, acc = tie((table, acc))
        moves = (2, 3) if k == 0 else (1, 2, 3)
        if k == 0:
            both = jnp.concatenate([group_moments, table], axis=0)
            partner = lax.ppermute(both, "leaf", [(i, i ^ 1) for i in range(leaves)])
            pairs = [(i, i + 1 if i % 2 else i - 1) for i in range(1, leaves - 1)]
            side = lax.ppermute(group_moments, "leaf", pairs)
        others = [
            lax.ppermute(table, "leaf", [(i, i ^ (m << 2 * k)) for i in range(leaves)])
            for m in moves
        ]
        if k == 0:
            acc, src_c, src_q = near_first(
                share_of(k), plan_all, (left, mine, right), acc, group_size
            )
            others, partner, side, acc = tie((others, partner, side, acc))
            others = [partner[group_boxes:]] + list(others)
            partner = partner[:group_boxes]
        else:
            acc = near_next(share_of(k), plan_all, src_c, src_q, acc)
        if k == 1:
            box_far = box_field(picks, side, group_moments, partner, coupling2)
        table = jnp.concatenate([table] + list(others), axis=0)
    flips = jnp.where(far3_list[0] >= 0, far3_list[0] ^ group, -1)
    lane_box = (lane * clusters)[None]
    return go_down(
        flips,
        own_counts,
        lane_box,
        table,
        coupling3[0],
        transfer2,
        box_far,
        transfer1,
        basis,
        acc,
    )


def solution(mesh):
    return jax.shard_map(
        on_device,
        mesh=mesh,
        in_specs=(
            P("leaf", None, None),
            P(("leaf", "sub"), None, None),
            P("leaf"),
            P("leaf"),
            P(("leaf", "sub"), None),
            P(("leaf", "sub"), None, None),
            P(("leaf", "sub"), None, None),
            P(("leaf", "sub"), None),
            P(("leaf", "sub"), None, None, None),
            P("leaf", None, None),
            P("leaf", None),
            P("leaf", None, None, None),
        ),
        out_specs=P(("leaf", "sub"), None, None),
        check_vma=False,
    )
```

```python
import functools

import jax
import jax.numpy as jnp
from jax import lax
from jax.experimental import pallas as pl
from jax.experimental.pallas import tpu as pltpu
from jax.sharding import PartitionSpec as P

kernel_scale = 0.07957747154594767
delta_squared = 0.0025

SLOTS = 4
UNITS = 16
STRIDE = 32
CLASSES = (128, 96, 64)
COSTS = (5, 4, 3)
OWN_UNITS = 2
VMEM_LIMIT = 36 << 20

in_vmem = pl.BlockSpec(memory_space=pltpu.VMEM)
in_place = pl.BlockSpec(memory_space=pl.ANY)


def shift(x, axis, by):
    count = lax.axis_size(axis)
    return lax.ppermute(x, axis, [(i, (i + by) % count) for i in range(count)])


def slide(x, axis, by):
    count = lax.axis_size(axis)
    pairs = [(i, i + by) for i in range(count) if 0 <= i + by < count]
    return lax.ppermute(x, axis, pairs)


def gather_ring(x, axis):
    count = lax.axis_size(axis)
    return [x] + [shift(x, axis, -k) for k in range(1, count)]


def prepare_targets(low, count, order, first, src_c, tile_t):
    pick = lax.broadcasted_iota(jnp.int32, (8, 256), 1) // 128
    pick = (pick == lax.broadcasted_iota(jnp.int32, (8, 256), 0)).astype(jnp.bfloat16)
    line = lax.broadcasted_iota(jnp.int32, (8, 128), 0)
    targets = order.shape[0]

    def body(w, _):
        for j in range(8):
            row = w * 8 + j
            at = first + order[jnp.minimum(low + row, targets - 1)]
            x = [jnp.broadcast_to(src_c[c, pl.ds(at, 1), :], (8, 128)) for c in range(3)]
            x = jnp.where(line == 0, x[0], jnp.where(line == 1, x[1], x[2])).T
            wide = jnp.dot(x.astype(jnp.bfloat16), pick, preferred_element_type=jnp.float32)
            tile_t[row * 3] = wide[:, :128]
            tile_t[row * 3 + 1] = wide[:, 128:]
            tile_t[row * 3 + 2] = jnp.broadcast_to(x[:, 2:3], (128, 128))
        return 0

    lax.fori_loop(0, (count + 7) // 8, body, 0)
    for c in range(3):
        tile_t[targets * 3 + c] = jnp.zeros((128, 128), jnp.float32)


def arrange_kernel(place, counts, b0, b1, b2, b3, coords, out_ref, held, sems):
    rows = b0.shape[0]
    leaves = place.shape[0]
    copies = [
        pltpu.make_async_copy(b, held.at[pl.ds(k * rows, rows)], sems.at[k])
        for k, b in enumerate((b0, b1, b2, b3))
    ]
    for copy in copies:
        copy.start()
    for copy in copies:
        copy.wait()
    point = lax.broadcasted_iota(jnp.int32, (8, 128), 1)

    def body(w, _):
        for j in range(16):
            s = w * 16 + j
            row = held[place[s]].astype(jnp.float32)
            out_ref[s] = jnp.where(point < counts[s], row, 0.0).astype(jnp.bfloat16)
        return 0

    out_ref[leaves:] = coords[...]
    lax.fori_loop(0, leaves // 16, body, 0)


def arrange(place, counts, blocks, planes):
    leaves = place.shape[0]
    coords = planes.reshape(-1, 8, 128)
    whole = pl.BlockSpec(memory_space=pl.ANY)
    return pl.pallas_call(
        arrange_kernel,
        out_shape=jax.ShapeDtypeStruct((leaves + coords.shape[0], 8, 128), jnp.bfloat16),
        grid_spec=pltpu.PrefetchScalarGridSpec(
            num_scalar_prefetch=2,
            grid=(),
            in_specs=[whole] * 4 + [in_vmem],
            out_specs=in_vmem,
            scratch_shapes=[
                pltpu.VMEM((leaves, 8, 128), jnp.bfloat16),
                pltpu.SemaphoreType.DMA((4,)),
            ],
        ),
        compiler_params=pltpu.CompilerParams(vmem_limit_bytes=8 << 20),
        cost_estimate=pl.CostEstimate(flops=1 << 20, bytes_accessed=2 << 20, transcendentals=0),
        name="arrange",
    )(place, counts, *blocks, coords)


def split(bounds, part, parts):
    left = jnp.int32(0)
    for k, cost in enumerate(COSTS):
        left = left + (bounds[k + 1] - bounds[k]) * cost
    left = left * part // parts
    at = jnp.int32(0)
    for k, cost in enumerate(COSTS):
        number = bounds[k + 1] - bounds[k]
        take = jnp.minimum(left // cost, number)
        at = at + take
        left = jnp.where(take == number, left - take * cost, 0)
    return at


def near_steps(plan, low, high, first_own, tile_t, src_c, src_q, acc, away):
    words, lists, bounds, ranks, order = plan
    bf = jnp.bfloat16
    targets = order.shape[0]

    def rank_of(u):
        return ranks[lax.shift_right_logical(words[u], 5)]

    end = jnp.minimum(high * UNITS, bounds[4])
    some = end > low * UNITS
    base = jnp.where(some, rank_of(jnp.where(some, low * UNITS, 0)), 0)
    count = jnp.where(some, rank_of(jnp.where(some, end - 1, 0)) + 1 - base, 0)
    prepare_targets(base, count, order, first_own, src_c, tile_t)

    def unit(word, rows):
        t = lax.shift_right_logical(word, 5)
        at = 3 * jnp.clip(ranks[t] - base, 0, targets)
        ids = [lists[word + k] - away for k in range(SLOTS)]
        charge = jnp.concatenate([src_q[i] for i in ids], axis=1)
        target = [
            [tile_t[at + c, 16 * m : 16 * m + 16, :].astype(bf) for c in range(3)]
            for m in range(rows // 16)
        ]
        columns = []
        for i in ids:
            source = [
                jnp.broadcast_to(src_c[c, pl.ds(i, 1), :], (16, 128)).astype(bf)
                for c in range(3)
            ]
            pieces = []
            for m in range(rows // 16):
                squared = None
                for c in range(3):
                    offset = target[m][c] - source[c]
                    if squared is None:
                        squared = offset * offset + jnp.asarray(delta_squared, bf)
                    else:
                        squared = squared + offset * offset
                pieces.append(lax.rsqrt(squared))
            columns.append(jnp.concatenate(pieces, axis=0))
        tile = jnp.concatenate(columns, axis=1)
        return t, lax.dot_general(
            charge, tile, (((1,), (1,)), ((), ())), preferred_element_type=jnp.float32
        )

    def step(rows, w, _):
        done = [unit(words[w * UNITS + j], rows) for j in range(UNITS)]
        for t, part in done:
            if rows < 128:
                part = jnp.concatenate([part, jnp.zeros((8, 128 - rows), jnp.float32)], axis=1)
            acc[t] = acc[t] + part * kernel_scale
        return 0

    for k, rows in enumerate(CLASSES):
        first = jnp.maximum(bounds[k], low)
        last = jnp.minimum(bounds[k + 1], high)
        lax.fori_loop(first, jnp.maximum(first, last), functools.partial(step, rows), 0)


def near_own_kernel(share, w, l, b, r, o, c_ref, q_ref, acc, tile_t, src_c, src_q, sem):
    group = c_ref.shape[1]
    copy = pltpu.make_async_copy(q_ref.at[pl.ds(0, group)], src_q.at[pl.ds(0, group)], sem)
    copy.start()
    src_q[group] = jnp.zeros(src_q.shape[1:], src_q.dtype)
    for c in range(3):
        src_c[c, :group, :] = c_ref[c].astype(jnp.float32)
        src_c[c, group:, :] = jnp.zeros((8, 128), jnp.float32)
    acc[...] = jnp.zeros_like(acc)
    copy.wait()
    near_steps((w, l, b, r, o), 0, b[3], share[0], tile_t, src_c, src_q, acc, group)


def near_first_kernel(
    parts, share, w, l, b, r, o, x0, x1, x2, acc_in, acc, src_c, src_q, tile_t, stage, sems
):
    packs = (x0, x1, x2)
    eights = stage.shape[1]
    group = x0.shape[0] - eights
    copies = [
        pltpu.make_async_copy(x.at[pl.ds(group, eights)], stage.at[k], sems.at[k, 0])
        for k, x in enumerate(packs)
    ] + [
        pltpu.make_async_copy(
            x.at[pl.ds(0, group)], src_q.at[pl.ds(k * group, group)], sems.at[k, 1]
        )
        for k, x in enumerate(packs)
    ]
    for copy in copies:
        copy.start()
    src_q[3 * group] = jnp.zeros(src_q.shape[1:], src_q.dtype)
    acc[...] = acc_in[...]
    for copy in copies[:3]:
        copy.wait()
    for c in range(3):
        src_c[c, 3 * group :, :] = jnp.zeros((8, 128), jnp.float32)

        def spread(w, _):
            for k in range(3):
                for j in range(4):
                    i = w * 4 + j
                    rows = pl.ds(pl.multiple_of(k * group + 8 * i, 8), 8)
                    src_c[c, rows, :] = stage[k, c * (group // 8) + i].astype(jnp.float32)
            return 0

        lax.fori_loop(0, group // 32, spread, 0)
    for copy in copies[3:]:
        copy.wait()
    high = split(b, 1, parts)
    near_steps((w, l, b, r, o), 0, high, group + share[0], tile_t, src_c, src_q, acc, 0)


def near_next_kernel(part, parts, share, w, l, b, r, o, src_c, src_q, acc_in, acc, tile_t):
    group = src_q.shape[0] // 3
    acc[...] = acc_in[...]
    low = split(b, part, parts)
    high = split(b, part + 1, parts)
    near_steps((w, l, b, r, o), low, high, group + share[0], tile_t, src_c, src_q, acc, 0)


near_params = pltpu.CompilerParams(vmem_limit_bytes=VMEM_LIMIT)
near_cost = pl.CostEstimate(flops=1 << 32, bytes_accessed=1 << 20, transcendentals=50 << 20)


def tile_scratch(targets):
    return pltpu.VMEM((targets * 3 + 3, 128, 128), jnp.float32)


def near_own(share, plan, coords, charges, targets):
    group = coords.shape[1]
    return pl.pallas_call(
        near_own_kernel,
        out_shape=jax.ShapeDtypeStruct((targets + 1, 8, 128), jnp.float32),
        grid_spec=pltpu.PrefetchScalarGridSpec(
            num_scalar_prefetch=6,
            grid=(),
            in_specs=[in_vmem, in_place],
            out_specs=in_vmem,
            scratch_shapes=[
                tile_scratch(targets),
                pltpu.VMEM((3, group + 8, 128), jnp.float32),
                pltpu.VMEM((group + 1, 8, 128), jnp.bfloat16),
                pltpu.SemaphoreType.DMA,
            ],
        ),
        compiler_params=near_params,
        cost_estimate=near_cost,
        name="near_own",
    )(share, *plan, coords, charges)


def near_first(parts, share, plan, packs, acc, group):
    return pl.pallas_call(
        functools.partial(near_first_kernel, parts),
        out_shape=(
            jax.ShapeDtypeStruct(acc.shape, jnp.float32),
            pltpu.VMEM((3, 3 * group + 8, 128), jnp.float32),
            pltpu.VMEM((3 * group + 1, 8, 128), jnp.bfloat16),
        ),
        grid_spec=pltpu.PrefetchScalarGridSpec(
            num_scalar_prefetch=6,
            grid=(),
            in_specs=[in_place] * 3 + [in_vmem],
            out_specs=(in_vmem,) * 3,
            scratch_shapes=[
                tile_scratch(acc.shape[0] - 1),
                pltpu.VMEM((3, packs[0].shape[0] - group, 8, 128), jnp.bfloat16),
                pltpu.SemaphoreType.DMA((3, 2)),
            ],
        ),
        compiler_params=near_params,
        cost_estimate=near_cost,
        name="near_first",
    )(share, *plan, *packs, acc)


def near_next(part, parts, share, plan, src_c, src_q, acc):
    return pl.pallas_call(
        functools.partial(near_next_kernel, part, parts),
        out_shape=jax.ShapeDtypeStruct(acc.shape, jnp.float32),
        grid_spec=pltpu.PrefetchScalarGridSpec(
            num_scalar_prefetch=6,
            grid=(),
            in_specs=[in_vmem] * 3,
            out_specs=in_vmem,
            scratch_shapes=[tile_scratch(acc.shape[0] - 1)],
        ),
        compiler_params=near_params,
        cost_estimate=near_cost,
        name="near_next",
    )(share, *plan, src_c, src_q, acc)


def boxes_kernel(picks, left, mine, right, couple, out_ref, table):
    boxes, rhs, rank = out_ref.shape
    group = mine.shape[0]
    slots = picks.shape[0] // boxes
    for k, ref in enumerate((left, mine, right)):
        part = ref[...].astype(jnp.float32)
        table[k * group : (k + 1) * group] = jnp.concatenate([part, part], axis=2)
    table[3 * group] = jnp.zeros((rhs, 2 * rank), jnp.float32)
    low = lax.broadcasted_iota(jnp.int32, (rhs, 2 * rank), 1) < rank

    def body(w, _):
        for j in range(4):
            b = w * 4 + j
            total = jnp.zeros((rhs, rank), jnp.float32)
            for k in range(0, slots, 4):
                at = [table[picks[b * slots + k + i]] for i in range(4)]
                lhs = jnp.concatenate(
                    [jnp.where(low, at[0], at[1]), jnp.where(low, at[2], at[3])], axis=1
                )
                rhs_block = couple[pl.ds(b * slots + k, 4)].reshape(4 * rank, rank)
                total = total + jnp.dot(
                    lhs.astype(jnp.bfloat16), rhs_block, preferred_element_type=jnp.float32
                )
            out_ref[b] = total
        return 0

    lax.fori_loop(0, boxes // 4, body, 0)


def box_field(picks, left, mine, right, couple):
    boxes, slots, rank, _ = couple.shape
    rhs = mine.shape[1]
    return pl.pallas_call(
        boxes_kernel,
        out_shape=jax.ShapeDtypeStruct((boxes, rhs, rank), jnp.float32),
        grid_spec=pltpu.PrefetchScalarGridSpec(
            num_scalar_prefetch=1,
            grid=(),
            in_specs=[in_vmem] * 4,
            out_specs=in_vmem,
            scratch_shapes=[pltpu.VMEM((3 * mine.shape[0] + 1, rhs, 2 * rank), jnp.float32)],
        ),
        compiler_params=pltpu.CompilerParams(vmem_limit_bytes=12 << 20),
        cost_estimate=pl.CostEstimate(flops=1 << 24, bytes_accessed=4 << 20, transcendentals=0),
        name="box_field",
    )(picks, left, mine, right, couple.reshape(boxes * slots, rank, rank))


def down_kernel(flips, counts, share, table, c3, t2, box_far, t1, basis, near, out_ref, local):
    boxes, rhs, rank = box_far.shape
    leaves = out_ref.shape[0]
    bf = jnp.bfloat16
    across = (((1,), (1,)), ((), ()))
    top = jnp.zeros((rhs, rank), jnp.float32)
    for k in range(flips.shape[0]):
        at = flips[k]
        source = table[jnp.maximum(at, 0)].astype(jnp.float32)
        source = jnp.where(at >= 0, source, jnp.zeros_like(source)).astype(bf)
        top = top + jnp.dot(source, c3[k], preferred_element_type=jnp.float32)
    top = top.astype(bf)
    for b in range(boxes):
        part = lax.dot_general(top, t2[share[0] + b], across, preferred_element_type=jnp.float32)
        local[b] = (box_far[b] + part).astype(bf)
    point = lax.broadcasted_iota(jnp.int32, (rhs, 128), 1)
    fan = leaves // boxes

    def body(w, _):
        first = w * 2 * fan
        moments = [
            lax.dot_general(
                local[w * 2 + j // fan], t1[first + j], across, preferred_element_type=jnp.float32
            ).astype(bf)
            for j in range(2 * fan)
        ]
        fars = [
            jnp.dot(moments[j], basis[first + j], preferred_element_type=jnp.float32)
            for j in range(2 * fan)
        ]
        for j in range(2 * fan):
            t = first + j
            out_ref[t] = jnp.where(point < counts[t], near[t] + fars[j], 0.0)
        return 0

    lax.fori_loop(0, boxes // 2, body, 0)


def go_down(flips, counts, share, table, c3, t2, box_far, t1, basis, near):
    leaves = counts.shape[0]
    return pl.pallas_call(
        down_kernel,
        out_shape=jax.ShapeDtypeStruct((leaves,) + near.shape[1:], jnp.float32),
        grid_spec=pltpu.PrefetchScalarGridSpec(
            num_scalar_prefetch=3,
            grid=(),
            in_specs=[in_vmem] * 7,
            out_specs=in_vmem,
            scratch_shapes=[pltpu.VMEM(box_far.shape, jnp.bfloat16)],
        ),
        compiler_params=pltpu.CompilerParams(vmem_limit_bytes=16 << 20),
        cost_estimate=pl.CostEstimate(flops=1 << 26, bytes_accessed=5 << 20, transcendentals=0),
        name="go_down",
    )(flips, counts, share, table, c3, t2, box_far, t1, basis, near)


def order_units(first, number, kind, targets, most):
    ids = jnp.arange(targets, dtype=jnp.int32)
    before = (kind[None, :] < kind[:, None]) | (
        (kind[None, :] == kind[:, None]) & (ids[None, :] < ids[:, None])
    )
    start = jnp.sum(jnp.where(before, number[None, :], 0), axis=1)
    classes = jnp.arange(len(CLASSES), dtype=jnp.int32)
    upto = jnp.sum(jnp.where(kind[None, :] <= classes[:, None], number[None, :], 0), axis=1)
    bounds = jnp.concatenate([jnp.zeros((1,), jnp.int32), (upto + UNITS - 1) // UNITS, upto[-1:]])
    unit = jnp.arange(most, dtype=jnp.int32)
    at = unit[:, None] - start[None, :]
    mine = (at >= 0) & (at < number[None, :])
    words = ids[None, :] * STRIDE + (first[None, :] + at) * SLOTS - targets * STRIDE
    return jnp.sum(jnp.where(mine, words, 0), axis=1) + targets * STRIDE, bounds


def plan_near(near_list, base, group, counts):
    targets, slots = near_list.shape
    dummy = 3 * group
    live = near_list >= 0
    local = jnp.where(live, jnp.clip(near_list - base, 0, dummy - 1), dummy)
    own = live & (local >= group) & (local < 2 * group)
    rest = live & ~own
    earlier = jnp.arange(slots)[:, None] < jnp.arange(slots)[None, :]
    own_number = jnp.sum(own, axis=1, dtype=jnp.int32)
    number = jnp.sum(live, axis=1, dtype=jnp.int32)
    own_rank = jnp.sum(own[:, :, None] & earlier[None], axis=1, dtype=jnp.int32)
    rest_rank = jnp.sum(rest[:, :, None] & earlier[None], axis=1, dtype=jnp.int32)
    rank = jnp.where(own, own_rank, jnp.where(rest, own_number[:, None] + rest_rank, STRIDE))
    slot = jnp.arange(STRIDE, dtype=jnp.int32)
    hit = rank[:, None, :] == slot[None, :, None]
    lists = jnp.sum(jnp.where(hit, local[:, None, :] - dummy, 0), axis=2) + dummy
    lists = jnp.pad(lists, ((0, 1), (0, 0)), constant_values=dummy).reshape(-1)
    kind = sum((counts <= rows).astype(jnp.int32) for rows in CLASSES[1:])
    whole = jnp.minimum(own_number // SLOTS, OWN_UNITS)
    units = (number + SLOTS - 1) // SLOTS
    most = targets * ((slots + SLOTS - 1) // SLOTS) + UNITS
    zero = jnp.zeros_like(whole)
    words_own, bounds_own = order_units(zero, whole, kind, targets, most)
    words_all, bounds_all = order_units(whole, units - whole, kind, targets, most)
    lists_own = jnp.where(lists == dummy, 2 * group, lists)
    ids = jnp.arange(targets, dtype=jnp.int32)
    before = (kind[None, :] < kind[:, None]) | (
        (kind[None, :] == kind[:, None]) & (ids[None, :] < ids[:, None])
    )
    ranks = jnp.sum(before, axis=1, dtype=jnp.int32)
    order = jnp.sum(jnp.where(ranks[None, :] == ids[:, None], ids[None, :], 0), axis=1)
    ranks = jnp.pad(ranks, (0, 1), constant_values=4 * targets)
    return (words_own, lists_own, bounds_own, ranks, order), (
        words_all,
        lists,
        bounds_all,
        ranks,
        order,
    )


def on_device(
    coords,
    charges,
    counts,
    morton,
    near_list,
    basis,
    transfer1,
    far2_list,
    coupling2,
    transfer2,
    far3_list,
    coupling3,
):
    lane = lax.axis_index("sub")
    group = lax.axis_index("leaf")
    leaves = lax.axis_size("leaf")
    lanes = lax.axis_size("sub")
    leaf_dev, rhs_count, points = charges.shape
    rank_size = basis.shape[1]
    group_size = coords.shape[0]
    clusters = far2_list.shape[0]
    group_boxes = transfer2.shape[0]
    start = lane * leaf_dev

    tie = lax.optimization_barrier

    blocks = gather_ring(charges, "sub")
    planes = jnp.transpose(coords, (1, 0, 2))
    own_counts = lax.dynamic_slice_in_dim(counts, start, leaf_dev, 0)

    slot = jnp.arange(group_size, dtype=jnp.int32)
    inverse = jnp.sum(jnp.where(morton[None, :] == slot[:, None], slot[None, :], 0), axis=1)
    place = lax.rem(inverse // leaf_dev - lane + lanes, lanes) * leaf_dev + inverse % leaf_dev
    plan_own, plan_all = plan_near(near_list, (group - 1) * group_size, group_size, own_counts)

    blocks, plan_own, plan_all = tie((blocks, plan_own, plan_all))
    mine = arrange(place, counts, blocks, planes)
    left = slide(mine, "leaf", 1)
    right = slide(mine, "leaf", -1)

    own_charges = lax.dynamic_slice_in_dim(mine, start, leaf_dev, 0)
    transfer_boxed = transfer1.reshape(clusters, 8, rank_size, rank_size)
    leaf_moments = jnp.einsum(
        "trp,tkp->trk", own_charges, basis, preferred_element_type=jnp.float32
    ).astype(jnp.bfloat16)
    box_moments = jnp.einsum(
        "bnrc,bncp->brp",
        leaf_moments.reshape(clusters, 8, rhs_count, rank_size),
        transfer_boxed,
        preferred_element_type=jnp.float32,
    ).astype(jnp.bfloat16)

    rounds = (leaves.bit_length() - 1) // 2

    share = start[None]
    mine_after, box_moments = tie((mine, box_moments))
    ring = gather_ring(box_moments, "sub")
    acc = near_own(share, plan_own, planes, mine_after, leaf_dev)
    ring, acc = tie((ring, acc))
    group_moments = jnp.roll(jnp.stack(ring), lane, axis=0)
    group_moments = group_moments.reshape(group_boxes, rhs_count, rank_size)
    top_moment = jnp.einsum(
        "brc,bcp->rp", group_moments, transfer2, preferred_element_type=jnp.float32
    ).astype(jnp.bfloat16)

    far2_local = jnp.clip(far2_list - (group - 1) * group_boxes, 0, 3 * group_boxes - 1)
    odd = lax.rem(group, 2) == 1
    block = far2_local // group_boxes
    block = jnp.where(odd, 2 - block, block)
    far2_local = block * group_boxes + far2_local % group_boxes
    picks = jnp.where(far2_list >= 0, far2_local, 3 * group_boxes).reshape(-1)
    table = top_moment[None]
    box_far = None
    for k in range(rounds):
        if k == rounds - 1:
            table, acc, box_far = tie((table, acc, box_far))
        else:
            table, acc = tie((table, acc))
        moves = (2, 3) if k == 0 else (1, 2, 3)
        if k == 0:
            both = jnp.concatenate([group_moments, table], axis=0)
            partner = lax.ppermute(both, "leaf", [(i, i ^ 1) for i in range(leaves)])
            pairs = [(i, i + 1 if i % 2 else i - 1) for i in range(1, leaves - 1)]
            side = lax.ppermute(group_moments, "leaf", pairs)
        others = [
            lax.ppermute(table, "leaf", [(i, i ^ (m << 2 * k)) for i in range(leaves)])
            for m in moves
        ]
        if k == 0:
            acc, src_c, src_q = near_first(
                rounds, share, plan_all, (left, mine, right), acc, group_size
            )
            others, partner, side, acc = tie((others, partner, side, acc))
            others = [partner[group_boxes:]] + list(others)
            partner = partner[:group_boxes]
        else:
            acc = near_next(k, rounds, share, plan_all, src_c, src_q, acc)
        if k == 1:
            box_far = box_field(picks, side, group_moments, partner, coupling2)
        table = jnp.concatenate([table] + list(others), axis=0)
    flips = jnp.where(far3_list[0] >= 0, far3_list[0] ^ group, -1)
    lane_box = (lane * clusters)[None]
    return go_down(
        flips,
        own_counts,
        lane_box,
        table,
        coupling3[0],
        transfer2,
        box_far,
        transfer1,
        basis,
        acc,
    )


def solution(mesh):
    return jax.shard_map(
        on_device,
        mesh=mesh,
        in_specs=(
            P("leaf", None, None),
            P(("leaf", "sub"), None, None),
            P("leaf"),
            P("leaf"),
            P(("leaf", "sub"), None),
            P(("leaf", "sub"), None, None),
            P(("leaf", "sub"), None, None),
            P(("leaf", "sub"), None),
            P(("leaf", "sub"), None, None, None),
            P("leaf", None, None),
            P("leaf", None),
            P("leaf", None, None, None),
        ),
        out_specs=P(("leaf", "sub"), None, None),
        check_vma=False,
    )
```
